256 devices in a mesh: ctx: 8 (over z_hi, core), vocab: 32 (over x, y, z_lo).
Axes of the slice: x: 4, y: 4, z: 8 (z_hi: 4, z_lo: 2; z = z_hi * 2 + z_lo), core: 2. Of those that a mesh axis runs over, the one named last changes fastest.
Arguments:
- hidden: bfloat16 [512, 2, 7168], P('ctx', None, 'vocab'), may hold values from -30 to 30
- head: bfloat16 [7168, 65536], P('ctx', 'vocab'), may hold values from -0.15 to 0.15
- targets: int32 [512, 2], P('ctx'), may hold values from 0 to 65535
- loss_weight: float32 [512, 2], P('ctx'), may hold values from 16 to 256
Outputs:
- token_loss: float32 [512, 2], P('ctx')
- grad_hidden: bfloat16 [512, 2, 7168], P('ctx', None, 'vocab')
The draws below stay inside these ranges and needn't reach their ends.
All inputs are finite; a program needn't handle non-finite values.
Results may differ from the reference program's by a relative error of at most 0.0046.
Values may be sent and summed in bfloat16 or wider, within the bound.
A program may use at most 64 MiB of HBM per device.

```python
import math
import jax
import jax.numpy as jnp
import numpy as np
from jax import lax

D = 7168
DEPTHS = 2
TOKENS = 512
VOCAB = 65536


def draw_hidden(key, part):
    draw_base = jnp.clip(jax.random.normal(jax.random.fold_in(key, 1), (TOKENS, DEPTHS, D), jnp.float32), -6.0, 6.0)
    return draw_base.astype(jnp.bfloat16)


def draw_head(key, part):
    scale_col = D ** (-0.5)
    draw_base = jnp.clip(jax.random.normal(jax.random.fold_in(key, 4), (D, VOCAB), jnp.float32), -6.0, 6.0) * scale_col
    draw_base = jnp.clip(draw_base, -0.149, 0.149)
    return draw_base.astype(jnp.bfloat16)


def touch_ends(values, own_key, least, high):
    index_at = [jax.random.randint(jax.random.fold_in(own_key, axis), (), 0, length) for axis, length in enumerate(values.shape)]
    main_axis = values.shape.index(max(values.shape))
    next_to = index_at[:main_axis] + [(index_at[main_axis] + 1) % values.shape[main_axis]] + index_at[main_axis + 1:]
    return values.at[tuple(index_at)].set(least).at[tuple(next_to)].set(high)


def levels(rng, dims, pieces, low, largest):
    level, own = 1.0, jax.random.fold_in(rng, 6)
    for axis_at, blocks in pieces:
        heights = jnp.exp(jax.random.uniform(jax.random.fold_in(own, axis_at), (blocks,), jnp.float32, low / len(pieces), largest / len(pieces)))
        level = level * jnp.repeat(heights, dims[axis_at] // blocks).reshape([-1 if axis == axis_at else 1 for axis in range(len(dims))])
    return level


def rank_table(count, slope):
    loads = [(1 << 20) // math.isqrt(standing ** slope) + 1 for standing in range(1, count + 1)]
    scale = 1 + sum(loads) // (1 << 30)
    return np.cumsum(np.array([max(1, weight // scale) for weight in loads]))


def skewed_ids(stream_key, dims, number_of, slope):
    grid = rank_table(number_of, slope)
    lot = jax.random.randint(jax.random.fold_in(stream_key, 1), dims, 0, int(grid[number_of - 1]))
    grade = jnp.searchsorted(jnp.asarray(grid, jnp.int32), lot, side="right")
    return jax.random.permutation(jax.random.fold_in(stream_key, 2), number_of)[grade].astype(jnp.int32)


def setup_inputs(seed: int = 0) -> dict:
    key_of = jax.random.split(jax.random.key(seed), 5)
    hidden = draw_hidden(jax.random.fold_in(key_of[4], 71), 0)
    head = draw_head(jax.random.fold_in(key_of[4], 71), 0)
    targets = touch_ends(skewed_ids(key_of[2], (TOKENS, DEPTHS), VOCAB, 2), jax.random.fold_in(key_of[2], 3), 0, VOCAB - 1).astype(jnp.int32)
    loss_weight = jnp.clip(jnp.exp(math.log(256.0) - 2.7725887 * jax.random.uniform(key_of[3], (TOKENS, DEPTHS), jnp.float32) ** levels(key_of[3], (TOKENS, DEPTHS), ((0, 8),), -0.2, 0.2)), 16.0, 256.0)
    return {"hidden": hidden, "head": head, "targets": targets, "loss_weight": loss_weight}


def reference(hidden, head, targets, loss_weight):
    flat_rows = hidden.reshape(TOKENS * DEPTHS, D)
    labels = targets.reshape(TOKENS * DEPTHS)
    weights = loss_weight.reshape(TOKENS * DEPTHS)
    logits = jnp.dot(flat_rows, head, preferred_element_type=jnp.float32)
    row_max = jnp.max(logits, axis=1)
    exps = jnp.exp(logits - row_max[:, None])
    sum_exp = jnp.sum(exps, axis=1)
    target_logit = jnp.take_along_axis(logits, labels[:, None], axis=1)[:, 0]
    token_loss = jnp.log(sum_exp) + row_max - target_logit
    columns = lax.broadcasted_iota(jnp.int32, logits.shape, 1)
    onehot = (columns == labels[:, None]).astype(jnp.float32)
    dlogits = (weights[:, None] * (exps / sum_exp[:, None] - onehot)).astype(jnp.bfloat16)
    grad_rows = jnp.dot(dlogits, head.T, preferred_element_type=jnp.float32).astype(jnp.bfloat16)
    return token_loss.reshape(TOKENS, DEPTHS), grad_rows.reshape(TOKENS, DEPTHS, D)
```

```python
import jax
import jax.numpy as jnp
from jax import lax
from jax.experimental import pallas as pl
from jax.experimental.pallas import tpu as pltpu
from jax.sharding import PartitionSpec as P

F32 = jnp.float32
BF16 = jnp.bfloat16
RING = 4
NV = 32
ROWS = 128
WIDTH = 224
VL = 2048
HV = VL // 2
SLAB = 4 * WIDTH


class Ring4Sum:
    def __init__(self, rdma, base, part, land, plus, minus, add):
        self.rdma, self.base, self.part, self.land = rdma, base, part, land
        self.plus, self.minus, self.add = plus, minus, add

    def copy(self, k):
        d, h, to_plus = ((2, 0, 0), (2, 1, 1), (3, 1, 0), (1, 0, 1), (3, 0, 0), (1, 1, 1))[k]
        dev = self.plus if to_plus else self.minus
        return self.rdma(self.part(d, h), self.land(k), self.base + k, dev)

    def start(self, *which):
        for k in which:
            self.copy(k).start()

    def relay(self):
        self.copy(0).wait_recv()
        self.add(self.part(3, 0), [self.land(0)])
        self.copy(4).start()
        self.copy(1).wait_recv()
        self.add(self.part(1, 1), [self.land(1)])
        self.copy(5).start()

    def arrive(self):
        for k in (2, 3, 4, 5):
            self.copy(k).wait_recv()

    def finish(self):
        self.arrive()
        self.add(self.part(0, 0), [self.land(3), self.land(4)])
        self.add(self.part(0, 1), [self.land(2), self.land(5)])

    def drain(self):
        for k in range(6):
            self.copy(k).wait_send()


def add_into(ref, others):
    total = ref[...]
    for o in others:
        total = total + o[...]
    ref[...] = total


def add_rows(ref, others):
    @pl.loop(0, ref.shape[0] // 16)
    def _(r):
        at = pl.ds(pl.multiple_of(r * 16, 16), 16)
        total = ref[at, :]
        for o in others:
            total = total + o[at, :]
        ref[at, :] = total


def kernel(
    hid,
    head_hbm,
    tgt,
    wgt,
    loss_out,
    grad_out,
    buf,
    head,
    part,
    pair,
    zland,
    logit,
    stat,
    msg,
    peers,
    dl,
    g,
    land1,
    land2,
    zbuf,
    obuf,
    obuf_in,
    ssem,
    rsem,
    st_s,
    st_r,
    lsem,
):
    c = lax.axis_index("ctx")
    v = lax.axis_index("vocab")
    zh, core = c // 2, c % 2
    x, y, zl = v // 8, (v // 2) % 4, v % 2

    def up(i, d):
        return (i + d) % RING

    def dev_zh(d):
        return (up(zh, d) * 2 + core, v)

    def dev_x(d):
        return (c, up(x, d) * 8 + y * 2 + zl)

    def dev_y(d):
        return (c, x * 8 + up(y, d) * 2 + zl)

    partner = (zh * 2 + 1 - core, v)
    dev_zl = (c, x * 8 + y * 2 + 1 - zl)
    swap = (v // 4, 4 * c + v % 4)
    is_self = v // 4 == c
    sv = 4 * c + v % 4

    def rdma(src, dst, i, dev):
        return pltpu.make_async_remote_copy(
            src_ref=src,
            dst_ref=dst,
            send_sem=ssem.at[i],
            recv_sem=rsem.at[i],
            device_id=dev,
            device_id_type=pl.DeviceIdType.MESH,
        )

    head_copy = pltpu.make_async_copy(head_hbm, head, lsem.at[0])
    head_copy.start()

    barrier = pltpu.get_barrier_semaphore()
    for dev in (
        partner,
        dev_zh(1),
        dev_zh(3),
        dev_x(1),
        dev_x(3),
        dev_y(1),
        dev_y(3),
        dev_zl,
    ):
        pl.semaphore_signal(barrier, inc=1, device_id=dev, device_id_type=pl.DeviceIdType.MESH)

    @pl.when(jnp.logical_not(is_self))
    def _():
        pl.semaphore_signal(barrier, inc=1, device_id=swap, device_id_type=pl.DeviceIdType.MESH)
        pl.semaphore_wait(barrier, 9)

    @pl.when(is_self)
    def _():
        pl.semaphore_wait(barrier, 8)

    @pl.when(is_self)
    def _():
        cp = pltpu.make_async_copy(hid, buf.at[x, y, zl], lsem.at[1])
        cp.start()
        cp.wait()

    @pl.when(jnp.logical_not(is_self))
    def _():
        cp = rdma(hid, buf.at[sv // 8, (sv // 2) % 4, sv % 2], 0, swap)
        cp.start()
        cp.wait_send()
        rdma(hid, buf.at[x, y, zl], 0, swap).wait_recv()

    z_out = rdma(buf.at[x, y, zl], buf.at[x, y, zl], 1, dev_zl)
    z_out.start()
    rdma(buf.at[x, y, zl], buf.at[x, y, 1 - zl], 1, dev_zl).wait_recv()

    lines = (
        (lambda a, b: buf.at[a, b, 0], x, y, dev_x, dev_y),
        (lambda a, b: buf.at[b, a, 1], y, x, dev_y, dev_x),
    )
    sends = [z_out]
    for k, (at, a, b, dev_a, dev_b) in enumerate(lines):
        base = 2 + 16 * k
        for d in (1, 3):
            cp = rdma(at(a, b), at(a, b), base + (0 if d == 1 else 1), dev_a(d))
            cp.start()
            sends.append(cp)
    steps = (0, 3, 1, 2)

    def second(k, n):
        at, a, b, dev_a, dev_b = lines[k]
        base = 2 + 16 * k
        for d, o in ((1, 4), (3, 8)):
            tile = at(up(a, steps[n]), b)
            cp = rdma(tile, tile, base + o + n, dev_b(d))
            cp.start()
            sends.append(cp)

    def second_in(k, n, d):
        at, a, b, dev_a, dev_b = lines[k]
        base = 2 + 16 * k
        tile = at(up(a, steps[n]), up(b, -d))
        rdma(tile, tile, base + (4 if d == 1 else 8) + n, dev_b(d)).wait_recv()
        return tile

    for k in (0, 1):
        second(k, 0)
    for k, (at, a, b, dev_a, dev_b) in enumerate(lines):
        base = 2 + 16 * k
        for d, i, rows in ((1, 0, pl.ds(0, 64)), (3, 1, pl.ds(64, 64))):
            tile = at(up(a, -d), b)
            rdma(tile, tile, base + i, dev_a(d)).wait_recv()
            half = tile.at[rows]
            cp = rdma(half, half, base + 2 + i, dev_a(d))
            cp.start()
            sends.append(cp)
            second(k, 1 + i)
    for k, (at, a, b, dev_a, dev_b) in enumerate(lines):
        base = 2 + 16 * k
        for d, i, rows in ((1, 0, pl.ds(0, 64)), (3, 1, pl.ds(64, 64))):
            half = at(up(a, 2), b).at[rows]
            rdma(half, half, base + 2 + i, dev_a(d)).wait_recv()
        second(k, 3)
    for n in (0, 1):
        for k, (at, a, b, dev_a, dev_b) in enumerate(lines):
            tile = second_in(k, n, 1)
            cp = rdma(tile, tile, 2 + 16 * k + 12 + n, dev_b(1))
            cp.start()
            sends.append(cp)
    for n in (2, 3):
        for k, (at, a, b, dev_a, dev_b) in enumerate(lines):
            tile = second_in(k, n, 3)
            cp = rdma(tile, tile, 2 + 16 * k + 12 + n, dev_b(3))
            cp.start()
            sends.append(cp)
    for k, (at, a, b, dev_a, dev_b) in enumerate(lines):
        for n in (2, 3):
            second_in(k, n, 1)
        for n in (0, 1):
            second_in(k, n, 3)
        for n in range(4):
            tile = at(up(a, steps[n]), up(b, 2))
            rdma(tile, tile, 2 + 16 * k + 12 + n, dev_b(1)).wait_recv()
    nsem = 34

    head_copy.wait()

    def forward(d):
        q = up(zh, d)

        @pl.loop(0, VL // 256)
        def _(n):
            cols = pl.ds(pl.multiple_of(n * 256, 256), 256)
            out_cols = pl.ds(pl.multiple_of((n % 4) * 256, 256), 256)
            acc = None
            for j in range(4):
                lhs = jnp.concatenate([buf[q, j // 2, j % 2], buf[q, 2 + j // 2, j % 2]], axis=0)
                term = jnp.dot(
                    lhs, head[j * WIDTH : (j + 1) * WIDTH, cols], preferred_element_type=F32
                )
                acc = term if acc is None else acc + term
            part[q, 0, n // 4, :, out_cols] = acc[:ROWS]
            part[q, 1, n // 4, :, out_cols] = acc[ROWS:]

    def pair_copy(d):
        q = up(zh, d)
        return rdma(part.at[q, 1 - core], pair.at[q], nsem + d, partner)

    def pair_add(d):
        q = up(zh, d)
        pair_copy(d).wait_recv()
        for h in (0, 1):
            add_rows(part.at[q, core, h], [pair.at[q, h]])

    zsum = Ring4Sum(
        rdma,
        nsem + 4,
        lambda d, h: part.at[up(zh, d), core, h],
        lambda k: zland.at[k],
        dev_zh(1),
        dev_zh(3),
        add_rows,
    )
    nsem2 = nsem + 10
    forward(2)
    pair_copy(2).start()
    forward(3)
    pair_copy(3).start()
    pair_add(2)
    zsum.start(0, 1)
    forward(1)
    pair_copy(1).start()
    pair_add(3)
    zsum.start(2)
    pair_add(1)
    zsum.start(3)
    forward(0)
    pair_copy(0).start()
    zsum.relay()
    pair_copy(0).wait_recv()
    zsum.arrive()

    lanes = lax.broadcasted_iota(jnp.int32, (16, 128), 1)
    cols0 = lax.broadcasted_iota(jnp.int32, (16, HV), 1) + v * VL

    @pl.loop(0, ROWS // 16)
    def _(r):
        at = pl.ds(pl.multiple_of(r * 16, 16), 16)
        t = tgt[at, :]
        l0 = part[zh, core, 0, at, :] + pair[zh, 0, at, :] + zland[3, at, :] + zland[4, at, :]
        l1 = part[zh, core, 1, at, :] + pair[zh, 1, at, :] + zland[2, at, :] + zland[5, at, :]
        top = jnp.maximum(jnp.max(l0, axis=1, keepdims=True), jnp.max(l1, axis=1, keepdims=True))
        hit = jnp.sum(jnp.where(cols0 == t, l0, 0.0), axis=1, keepdims=True) + jnp.sum(
            jnp.where(cols0 + HV == t, l1, 0.0), axis=1, keepdims=True
        )
        e0 = jnp.exp(l0 - top)
        e1 = jnp.exp(l1 - top)
        total = jnp.sum(e0, axis=1, keepdims=True) + jnp.sum(e1, axis=1, keepdims=True)
        logit[0, at, :] = e0
        logit[1, at, :] = e1
        stat[at, :] = jnp.where(lanes == 0, top, jnp.where(lanes == 1, total, hit))

    msg[...] = jnp.transpose(stat[...])[:8]

    def peer_copy(r):
        return pltpu.make_async_remote_copy(
            src_ref=msg,
            dst_ref=peers.at[r - 1],
            send_sem=st_s.at[r - 1],
            recv_sem=st_r.at[r - 1],
            device_id=(c, (v + r) % NV),
            device_id_type=pl.DeviceIdType.MESH,
        )

    @pl.loop(1, NV)
    def _(r):
        peer_copy(r).start()

    @pl.loop(1, NV)
    def _(r):
        peer_copy(r).wait_recv()

    top, total, hit = msg[0:1, :], msg[1:2, :], msg[2:3, :]
    best = jnp.maximum(top, jnp.max(peers[:, 0, :], axis=0, keepdims=True))
    everyone = total * jnp.exp(top - best) + jnp.sum(
        peers[:, 1, :] * jnp.exp(peers[:, 0, :] - best), axis=0, keepdims=True
    )
    hits = hit + jnp.sum(peers[:, 2, :], axis=0, keepdims=True)
    loss_out[...] = jnp.broadcast_to(jnp.log(everyone) + best - hits, (8, 128))
    scale = jnp.exp(top - best) / everyone
    stat[...] = jnp.transpose(jnp.broadcast_to(scale, (128, 128)))

    @pl.loop(0, ROWS // 16)
    def _(r):
        at = pl.ds(pl.multiple_of(r * 16, 16), 16)
        t = tgt[at, :]
        w = wgt[at, :]
        s = stat[at, 0:1]
        for h in (0, 1):
            one = (cols0 + h * HV == t).astype(F32)
            dl[zh, core, at, h * HV : (h + 1) * HV] = (w * (logit[h, at, :] * s - one)).astype(BF16)

    def across(slot, i, dev):
        return rdma(slot, slot, i, dev)

    own = dl.at[zh, core]
    top_half, low_half = pl.ds(0, 64), pl.ds(64, 64)
    ag = nsem2
    out = [across(own, ag, dev_zh(1)), across(own, ag + 1, dev_zh(3)), across(own, ag + 2, partner)]
    for cp in out:
        cp.start()

    def backward(d):
        q = up(zh, d)
        lhs = jnp.concatenate([dl[q, 0], dl[q, 1]], axis=0)
        for j in range(4):
            res = lax.dot_general(
                lhs,
                head[j * WIDTH : (j + 1) * WIDTH, :],
                (((1,), (1,)), ((), ())),
                preferred_element_type=F32,
            )
            g[q, j // 2, j % 2] = res[:ROWS]
            g[q, 2 + j // 2, j % 2] = res[ROWS:]

    def landed(d, k, i, rows=None):
        slot = dl.at[up(zh, d), k]
        if rows is not None:
            slot = slot.at[rows]
        across(slot, i, partner).wait_recv()
        return slot

    def onward(slot, i, dev):
        cp = across(slot, i, dev)
        cp.start()
        out.append(cp)

    landed(0, 1 - core, ag + 2)
    backward(0)
    slot = landed(3, core, ag)
    onward(slot.at[top_half], ag + 3, dev_zh(1))
    onward(slot, ag + 4, partner)
    slot = landed(1, core, ag + 1)
    onward(slot.at[low_half], ag + 5, dev_zh(3))
    onward(slot, ag + 6, partner)
    landed(3, 1 - core, ag + 4)
    backward(3)
    landed(1, 1 - core, ag + 6)
    backward(1)
    onward(landed(2, core, ag + 3, top_half), ag + 7, partner)
    onward(landed(2, core, ag + 5, low_half), ag + 8, partner)
    landed(2, 1 - core, ag + 7, top_half)
    landed(2, 1 - core, ag + 8, low_half)
    backward(2)

    rs = ag + 9
    first = [
        Ring4Sum(
            rdma,
            rs,
            lambda d, h: g.at[pl.ds(2 * h, 2), up(y, d), 0],
            lambda k: land1.at[0, k],
            dev_y(1),
            dev_y(3),
            add_into,
        ),
        Ring4Sum(
            rdma,
            rs + 6,
            lambda d, h: g.at[up(x, d), pl.ds(2 * h, 2), 1],
            lambda k: land1.at[1, k],
            dev_x(1),
            dev_x(3),
            add_into,
        ),
    ]
    then = [
        Ring4Sum(
            rdma,
            rs + 12,
            lambda d, h: g.at[up(x, d), y, 0, pl.ds(64 * h, 64)],
            lambda k: land2.at[0, k],
            dev_x(1),
            dev_x(3),
            add_into,
        ),
        Ring4Sum(
            rdma,
            rs + 18,
            lambda d, h: g.at[x, up(y, d), 1, pl.ds(64 * h, 64)],
            lambda k: land2.at[1, k],
            dev_y(1),
            dev_y(3),
            add_into,
        ),
    ]
    for stage in (first, then):
        for s in stage:
            s.start(0, 1, 2, 3)
        for s in stage:
            s.relay()
        for s in stage:
            s.finish()
    zi = rs + 24
    z_last = rdma(g.at[x, y, 1 - zl], zbuf, zi, dev_zl)
    z_last.start()
    z_last.wait_recv()
    obuf[...] = (g[x, y, zl] + zbuf[...]).astype(BF16)

    @pl.when(is_self)
    def _():
        cp = pltpu.make_async_copy(obuf, obuf_in, lsem.at[1])
        cp.start()
        cp.wait()

    @pl.when(jnp.logical_not(is_self))
    def _():
        cp = rdma(obuf, obuf_in, zi + 1, swap)
        cp.start()
        cp.wait()

    grad_out[...] = obuf_in[...]

    for cp in sends:
        cp.wait_send()
    for d in range(4):
        pair_copy(d).wait_send()
    zsum.drain()

    @pl.loop(1, NV)
    def _(r):
        peer_copy(r).wait_send()

    for cp in out:
        cp.wait_send()
    for s in first + then:
        s.drain()
    z_last.wait_send()


NSEM = 34 + 10 + 9 + 24 + 2


def body(hidden, head, targets, loss_weight):
    tile = (ROWS, WIDTH)
    vmem = pl.BlockSpec(memory_space=pltpu.VMEM)
    loss, grad = pl.pallas_call(
        kernel,
        out_shape=(
            jax.ShapeDtypeStruct((8, ROWS), F32),
            jax.ShapeDtypeStruct(tile, BF16),
        ),
        in_specs=[vmem, pl.BlockSpec(memory_space=pl.ANY), vmem, vmem],
        out_specs=(vmem, vmem),
        scratch_shapes=[
            pltpu.VMEM((RING, RING, 2, *tile), BF16),
            pltpu.VMEM((SLAB, VL), BF16),
            pltpu.VMEM((RING, 2, 2, ROWS, HV), F32),
            pltpu.VMEM((RING, 2, ROWS, HV), F32),
            pltpu.VMEM((6, ROWS, HV), F32),
            pltpu.VMEM((2, ROWS, HV), F32),
            pltpu.VMEM((ROWS, 128), F32),
            pltpu.VMEM((8, ROWS), F32),
            pltpu.VMEM((NV - 1, 8, ROWS), F32),
            pltpu.VMEM((RING, 2, ROWS, VL), BF16),
            pltpu.VMEM((RING, RING, 2, *tile), F32),
            pltpu.VMEM((2, 6, 2, *tile), F32),
            pltpu.VMEM((2, 6, ROWS // 2, WIDTH), F32),
            pltpu.VMEM(tile, F32),
            pltpu.VMEM(tile, BF16),
            pltpu.VMEM(tile, BF16),
            pltpu.SemaphoreType.DMA((NSEM,)),
            pltpu.SemaphoreType.DMA((NSEM,)),
            pltpu.SemaphoreType.DMA((NV - 1,)),
            pltpu.SemaphoreType.DMA((NV - 1,)),
            pltpu.SemaphoreType.DMA((2,)),
        ],
        compiler_params=pltpu.CompilerParams(
            collective_id=0, has_side_effects=True, vmem_limit_bytes=60 * 1024 * 1024
        ),
        name="mtp_loss",
    )(
        hidden.reshape(tile),
        head,
        targets.reshape(ROWS, 1),
        loss_weight.reshape(ROWS, 1),
    )
    rows, depths = targets.shape
    return loss[0].reshape(rows, depths), grad.reshape(rows, depths, WIDTH)


def solution(mesh):
    return jax.shard_map(
        body,
        mesh=mesh,
        in_specs=(P("ctx", None, "vocab"), P("ctx", "vocab"), P("ctx", None), P("ctx", None)),
        out_specs=(P("ctx", None), P("ctx", None, "vocab")),
        check_vma=False,
    )
```

```python
import jax
import jax.numpy as jnp
from jax import lax
from jax.experimental import pallas as pl
from jax.experimental.pallas import tpu as pltpu
from jax.sharding import PartitionSpec as P

F32 = jnp.float32
BF16 = jnp.bfloat16
RING = 4
NV = 32
ROWS = 128
WIDTH = 224
VL = 2048
HV = VL // 2
SLAB = 4 * WIDTH
NP = 2
RP = ROWS // NP
I16 = jnp.int16
LEVELS = 32766.0
HOPS = ((2, 0, 0), (2, 1, 1), (3, 1, 0), (1, 0, 1), (3, 0, 0), (1, 1, 1))


class Ring4Sum:
    def __init__(self, k, base, value, tiles, rows, block, coded, sides, plus, minus):
        self.k, self.base, self.value = k, base, value
        self.tiles, self.rows, self.block = tiles, rows, block
        (self.out, self.land), (self.sout, self.sland, self.cols) = coded, sides
        self.plus, self.minus = plus, minus

    def copies(self, i):
        dev = self.plus if HOPS[i][2] else self.minus
        b = self.base + 2 * i
        return (
            self.k.rdma(self.out.at[i], self.land.at[i], b, dev),
            self.k.rdma(self.sout.at[i], self.sland.at[i], b + 1, dev),
        )

    def send(self, i, landed=()):
        d, h, _ = HOPS[i]
        stat = self.k.stat
        lanes = lax.broadcasted_iota(jnp.int32, (self.block, 128), 1)

        @pl.loop(0, self.rows // self.block)
        def _(r):
            at = pl.ds(pl.multiple_of(r * self.block, self.block), self.block)
            side = jnp.zeros((self.block, 128), F32)
            for t in range(self.tiles):
                val = self.value(d, h, t, at)
                for j in landed:
                    val = val + self.decoded(j, t, at)
                low = jnp.min(val, axis=1, keepdims=True)
                high = jnp.max(val, axis=1, keepdims=True)
                middle = 0.5 * low + 0.5 * high
                span = jnp.maximum(0.5 * high - 0.5 * low, 1e-30)
                steps = jnp.clip(jnp.round((val - middle) * (LEVELS / span)), -LEVELS, LEVELS)
                self.out[i, t, at, :] = steps.astype(jnp.int32).astype(I16)
                side = jnp.where(lanes == 2 * t, middle, side)
                side = jnp.where(lanes == 2 * t + 1, span * (1.0 / LEVELS), side)
            stat[at, :] = side

        self.sout[i] = jnp.transpose(stat[...])[:8]
        for cp in self.copies(i):
            cp.start()
            self.k.pending.append(cp)

    def receive(self, i):
        for cp in self.copies(i):
            cp.wait_recv()
        rows = jnp.concatenate([self.sland[i]] * 16, axis=0)
        self.cols[i] = jnp.transpose(rows)

    def decoded(self, i, t, at):
        steps = self.land[i, t, at, :].astype(jnp.int32).astype(F32)
        return steps * self.cols[i, at, 2 * t + 1 : 2 * t + 2] + self.cols[i, at, 2 * t : 2 * t + 1]

    def relay(self):
        self.receive(0)
        self.send(4, (0,))
        self.receive(1)
        self.send(5, (1,))

    def arrive(self):
        for i in (2, 3, 4, 5):
            self.receive(i)

    def total(self, h, t, at):
        i, j = ((3, 4), (2, 5))[h]
        return self.value(0, h, t, at) + self.decoded(i, t, at) + self.decoded(j, t, at)


class Tools:
    def __init__(self, ssem, rsem, stat):
        self.ssem, self.rsem, self.stat, self.pending = ssem, rsem, stat, []

    def rdma(self, src, dst, i, dev):
        return pltpu.make_async_remote_copy(
            src_ref=src,
            dst_ref=dst,
            send_sem=self.ssem.at[i],
            recv_sem=self.rsem.at[i],
            device_id=dev,
            device_id_type=pl.DeviceIdType.MESH,
        )

    def start(self, src, dst, i, dev):
        cp = self.rdma(src, dst, i, dev)
        cp.start()
        self.pending.append(cp)


def kernel(
    hid,
    head_hbm,
    tgt,
    wgt,
    loss_out,
    grad_out,
    buf,
    head,
    part,
    pair,
    zcode,
    logit,
    stat,
    tcol,
    wcol,
    lcol,
    msg,
    peers,
    dl,
    g,
    code1,
    code2,
    sides,
    cols,
    zbuf,
    obuf,
    obuf_in,
    ssem,
    rsem,
    st_s,
    st_r,
    lsem,
):
    c = lax.axis_index("ctx")
    v = lax.axis_index("vocab")
    zh, core = c // 2, c % 2
    x, y, zl = v // 8, (v // 2) % 4, v % 2
    kit = Tools(ssem, rsem, stat)
    rdma, start = kit.rdma, kit.start

    def up(i, d):
        return (i + d) % RING

    def dev_zh(d):
        return (up(zh, d) * 2 + core, v)

    def dev_x(d):
        return (c, up(x, d) * 8 + y * 2 + zl)

    def dev_y(d):
        return (c, x * 8 + up(y, d) * 2 + zl)

    partner = (zh * 2 + 1 - core, v)
    dev_zl = (c, x * 8 + y * 2 + 1 - zl)
    hx, hy = up(x, zh), core * 2 + y % 2
    holder = (v // 4, hx * 8 + hy * 2 + zl)
    owner = (up(x, 4 - zh) * 2 + y // 2, 4 * c + v % 4)
    is_self = jnp.logical_and(holder[0] == c, holder[1] == v)

    head_copy = pltpu.make_async_copy(head_hbm, head, lsem.at[0])
    head_copy.start()

    barrier = pltpu.get_barrier_semaphore()

    def greet(dev):
        pl.semaphore_signal(barrier, inc=1, device_id=dev, device_id_type=pl.DeviceIdType.MESH)

    for dev in (
        partner,
        dev_zh(1),
        dev_zh(3),
        dev_x(1),
        dev_x(3),
        dev_y(1),
        dev_y(3),
        dev_zl,
    ):
        greet(dev)

    @pl.when(jnp.logical_not(is_self))
    def _():
        greet(holder)
        greet(owner)
        pl.semaphore_wait(barrier, 10)

    @pl.when(is_self)
    def _():
        pl.semaphore_wait(barrier, 8)

    @pl.when(is_self)
    def _():
        cp = pltpu.make_async_copy(hid, buf.at[x, y, zl], lsem.at[1])
        cp.start()
        cp.wait()

    @pl.when(jnp.logical_not(is_self))
    def _():
        cp = rdma(hid, buf.at[hx, hy, zl], 0, holder)
        cp.start()
        cp.wait_send()
        rdma(hid, buf.at[x, y, zl], 0, holder).wait_recv()

    start(buf.at[x, y, zl], buf.at[x, y, zl], 1, dev_zl)

    row = lax.broadcasted_iota(jnp.int32, (ROWS, ROWS // 2), 0)
    tok = lax.broadcasted_iota(jnp.int32, (ROWS, ROWS // 2), 1)

    def as_column(pairs):
        both = jnp.where(row % 2 == 1, pairs[1:2, :], pairs[0:1, :])
        return jnp.sum(jnp.where(row // 2 == tok, both, 0.0), axis=1, keepdims=True)

    tcol[...] = as_column(tgt[...].astype(F32)).astype(jnp.int32)
    wcol[...] = as_column(wgt[...])

    rdma(buf.at[x, y, zl], buf.at[x, y, 1 - zl], 1, dev_zl).wait_recv()

    lines = (
        (lambda a, b: buf.at[a, b, 0], x, y, dev_x, dev_y),
        (lambda a, b: buf.at[b, a, 1], y, x, dev_y, dev_x),
    )
    for k, (at, a, b, dev_a, dev_b) in enumerate(lines):
        base = 2 + 16 * k
        for d in (1, 3):
            start(at(a, b), at(a, b), base + (0 if d == 1 else 1), dev_a(d))
    steps = (0, 3, 1, 2)

    def second(k, n):
        at, a, b, dev_a, dev_b = lines[k]
        base = 2 + 16 * k
        for d, o in ((1, 4), (3, 8)):
            tile = at(up(a, steps[n]), b)
            start(tile, tile, base + o + n, dev_b(d))

    def second_in(k, n, d):
        at, a, b, dev_a, dev_b = lines[k]
        base = 2 + 16 * k
        tile = at(up(a, steps[n]), up(b, 4 - d))
        rdma(tile, tile, base + (4 if d == 1 else 8) + n, dev_b(d)).wait_recv()
        return tile

    for k in (0, 1):
        second(k, 0)
    for k, (at, a, b, dev_a, dev_b) in enumerate(lines):
        base = 2 + 16 * k
        for d, i, rows in ((1, 0, pl.ds(0, 64)), (3, 1, pl.ds(64, 64))):
            tile = at(up(a, 4 - d), b)
            rdma(tile, tile, base + i, dev_a(d)).wait_recv()
            half = tile.at[rows]
            start(half, half, base + 2 + i, dev_a(d))
            second(k, 1 + i)
    for k, (at, a, b, dev_a, dev_b) in enumerate(lines):
        base = 2 + 16 * k
        for d, i, rows in ((1, 0, pl.ds(0, 64)), (3, 1, pl.ds(64, 64))):
            half = at(up(a, 2), b).at[rows]
            rdma(half, half, base + 2 + i, dev_a(d)).wait_recv()
        second(k, 3)
    for n, d in ((0, 1), (1, 1), (2, 3), (3, 3)):
        for k, (at, a, b, dev_a, dev_b) in enumerate(lines):
            tile = second_in(k, n, d)
            start(tile, tile, 2 + 16 * k + 12 + n, dev_b(d))
    for k, (at, a, b, dev_a, dev_b) in enumerate(lines):
        for n, d in ((2, 1), (3, 1), (0, 3), (1, 3)):
            second_in(k, n, d)
        for n in range(4):
            tile = at(up(a, steps[n]), up(b, 2))
            rdma(tile, tile, 2 + 16 * k + 12 + n, dev_b(1)).wait_recv()
    sem = 34

    head_copy.wait()

    def forward(d):
        q = up(zh, d)
        at = up(q, zh)

        @pl.loop(0, VL // 256)
        def _(n):
            cs = pl.ds(pl.multiple_of(n * 256, 256), 256)
            out_cs = pl.ds(pl.multiple_of((n % 4) * 256, 256), 256)
            acc = None
            for j in range(4):
                lhs = jnp.concatenate([buf[at, j // 2, j % 2], buf[at, 2 + j // 2, j % 2]], axis=0)
                term = jnp.dot(
                    lhs, head[j * WIDTH : (j + 1) * WIDTH, cs], preferred_element_type=F32
                )
                acc = term if acc is None else acc + term
            for k in range(2):
                for p in range(NP):
                    lo = k * ROWS + p * RP
                    part[q, k, p, n // 4, :, out_cs] = acc[lo : lo + RP]

        for p in range(NP):
            start(part.at[q, 1 - core, p], pair.at[q, p], sem + d * NP + p, partner)

    def pair_in(d, p):
        q = up(zh, d)
        rdma(part.at[q, 1 - core, p], pair.at[q, p], sem + d * NP + p, partner).wait_recv()

    zr = [
        Ring4Sum(
            kit,
            sem + 4 * NP + 12 * p,
            lambda d, h, t, at, p=p: part[up(zh, d), core, p, h, at, :]
            + pair[up(zh, d), p, h, at, :],
            1,
            RP,
            16,
            (zcode.at[p, 0], zcode.at[p, 1]),
            (sides.at[p, 0, 0], sides.at[p, 0, 1], cols.at[0]),
            dev_zh(1),
            dev_zh(3),
        )
        for p in range(NP)
    ]
    forward(2)
    forward(3)
    pair_in(2, 0)
    zr[0].send(0)
    zr[0].send(1)
    forward(1)
    pair_in(3, 0)
    zr[0].send(2)
    pair_in(1, 0)
    zr[0].send(3)
    pair_in(2, 1)
    zr[1].send(0)
    zr[1].send(1)
    forward(0)
    zr[0].relay()
    pair_in(3, 1)
    zr[1].send(2)
    pair_in(1, 1)
    zr[1].send(3)
    zr[1].relay()
    sem2 = sem + 4 * NP + 12 * NP

    lanes = lax.broadcasted_iota(jnp.int32, (16, 128), 1)
    cols0 = lax.broadcasted_iota(jnp.int32, (16, HV), 1) + v * VL

    def peer_copy(p, r):
        return pltpu.make_async_remote_copy(
            src_ref=msg.at[p],
            dst_ref=peers.at[p, r - 1],
            send_sem=st_s.at[p, r - 1],
            recv_sem=st_r.at[p, r - 1],
            device_id=(c, (v + r) % NV),
            device_id_type=pl.DeviceIdType.MESH,
        )

    def softmax(p):
        pair_in(0, p)
        zr[p].arrive()

        @pl.loop(0, RP // 16)
        def _(r):
            at = pl.ds(pl.multiple_of(r * 16, 16), 16)
            t = tcol[pl.ds(pl.multiple_of(p * RP + r * 16, 16), 16), :]
            l0 = zr[p].total(0, 0, at)
            l1 = zr[p].total(1, 0, at)
            top = jnp.maximum(
                jnp.max(l0, axis=1, keepdims=True), jnp.max(l1, axis=1, keepdims=True)
            )
            hit = jnp.sum(jnp.where(cols0 == t, l0, 0.0), axis=1, keepdims=True) + jnp.sum(
                jnp.where(cols0 + HV == t, l1, 0.0), axis=1, keepdims=True
            )
            e0 = jnp.exp(l0 - top)
            e1 = jnp.exp(l1 - top)
            total = jnp.sum(e0, axis=1, keepdims=True) + jnp.sum(e1, axis=1, keepdims=True)
            logit[p, 0, at, :] = e0
            logit[p, 1, at, :] = e1
            stat[at, :] = jnp.where(lanes == 0, top, jnp.where(lanes == 1, total, hit))

        msg[p] = jnp.transpose(stat[...])[:8]

        @pl.loop(1, NV)
        def _(r):
            peer_copy(p, r).start()

    def gradient(p):
        @pl.loop(1, NV)
        def _(r):
            peer_copy(p, r).wait_recv()

        top, total, hit = msg[p, 0:1, :], msg[p, 1:2, :], msg[p, 2:3, :]
        tops = peers[p, :, 0, :]
        best = jnp.maximum(top, jnp.max(tops, axis=0, keepdims=True))
        everyone = total * jnp.exp(top - best) + jnp.sum(
            peers[p, :, 1, :] * jnp.exp(tops - best), axis=0, keepdims=True
        )
        hits = hit + jnp.sum(peers[p, :, 2, :], axis=0, keepdims=True)
        loss = jnp.log(everyone) + best - hits
        scale = jnp.exp(top - best) / everyone
        odd = lax.broadcasted_iota(jnp.int32, (128, 128), 0) % 2 == 1
        lcol[...] = jnp.transpose(jnp.where(odd, loss, scale))
        spot = lax.broadcasted_iota(jnp.int32, (RP, ROWS // 2), 1) * 2
        line = lax.broadcasted_iota(jnp.int32, (RP, ROWS // 2), 0) + p * RP
        for d in (0, 1):
            found = jnp.sum(
                jnp.where(line == spot + d, lcol[:RP, 1:2], 0.0), axis=0, keepdims=True
            )
            loss_out[d : d + 1, :] = found if p == 0 else loss_out[d : d + 1, :] + found

        @pl.loop(0, RP // 16)
        def _(r):
            at = pl.ds(pl.multiple_of(r * 16, 16), 16)
            here = pl.ds(pl.multiple_of(p * RP + r * 16, 16), 16)
            t = tcol[here, :]
            w = wcol[here, :]
            s = lcol[at, 0:1]
            for h in (0, 1):
                one = (cols0 + h * HV == t).astype(F32)
                dl[zh, core, here, h * HV : (h + 1) * HV] = (
                    w * (logit[p, h, at, :] * s - one)
                ).astype(BF16)

    class Gather:
        def __init__(self, p):
            self.p, self.base = p, sem2 + 9 * p
            self.all = pl.ds(p * RP, RP)
            self.first = pl.ds(p * RP, RP // 2)
            self.last = pl.ds(p * RP + RP // 2, RP // 2)

        def go(self, d, k, rows, i, dev):
            slot = dl.at[up(zh, d), k, rows]
            start(slot, slot, self.base + i, dev)

        def come(self, d, k, rows, i):
            slot = dl.at[up(zh, d), k, rows]
            rdma(slot, slot, self.base + i, partner).wait_recv()

        def begin(self):
            self.go(0, core, self.all, 0, dev_zh(1))
            self.go(0, core, self.all, 1, dev_zh(3))
            self.go(0, core, self.all, 2, partner)

        def near(self):
            self.come(3, core, self.all, 0)
            self.go(3, core, self.first, 3, dev_zh(1))
            self.come(1, core, self.all, 1)
            self.go(1, core, self.last, 5, dev_zh(3))
            self.go(3, core, self.all, 4, partner)
            self.go(1, core, self.all, 6, partner)

        def far(self):
            self.come(2, core, self.first, 3)
            self.go(2, core, self.first, 7, partner)
            self.come(2, core, self.last, 5)
            self.go(2, core, self.last, 8, partner)

        def backward(self, d):
            other = 1 - core
            if d == 2:
                self.come(2, other, self.first, 7)
                self.come(2, other, self.last, 8)
            else:
                self.come(d, other, self.all, {0: 2, 3: 4, 1: 6}[d])
            q = up(zh, d)
            at = up(q, zh)
            lhs = jnp.concatenate([dl[q, 0, self.all], dl[q, 1, self.all]], axis=0)
            for j in range(4):
                res = lax.dot_general(
                    lhs,
                    head[j * WIDTH : (j + 1) * WIDTH, :],
                    (((1,), (1,)), ((), ())),
                    preferred_element_type=F32,
                )
                g[at, j // 2, j % 2, self.all] = res[:RP]
                g[at, 2 + j // 2, j % 2, self.all] = res[RP:]

    class Collect:
        def __init__(self, p):
            self.p = p
            base = sem2 + 9 * NP + (48 + 2) * p
            self.base = base

            def here(at, lo=0):
                return pl.ds(pl.multiple_of(p * RP + lo + at.start, 16), at.size)

            self.here = here

            def ring(i, k, value, tiles, rows, code, dev):
                return Ring4Sum(
                    kit,
                    base + 12 * i,
                    value,
                    tiles,
                    rows,
                    16,
                    (code.at[p, k, 0], code.at[p, k, 1]),
                    (sides.at[p, 1 + i, 0], sides.at[p, 1 + i, 1], cols.at[1 + k]),
                    dev(1),
                    dev(3),
                )

            self.one = (
                ring(0, 0, lambda d, h, t, at: g[2 * h + t, up(y, d), 0, here(at), :], 2, RP, code1, dev_y),
                ring(1, 1, lambda d, h, t, at: g[up(x, d), 2 * h + t, 1, here(at), :], 2, RP, code1, dev_x),
            )
            half = RP // 2
            self.two = (
                ring(2, 0, lambda d, h, t, at: g[up(x, d), y, 0, here(at, half * h), :], 1, half, code2, dev_x),
                ring(3, 1, lambda d, h, t, at: g[x, up(y, d), 1, here(at, half * h), :], 1, half, code2, dev_y),
            )

        def begin(self, stage):
            for i in (0, 1, 2, 3):
                for s in stage:
                    s.send(i)

        def relay(self, stage):
            for s in stage:
                s.relay()

        def end_one(self):
            for k, s in enumerate(self.one):
                s.arrive()

                @pl.loop(0, RP // 16)
                def _(r):
                    at = pl.ds(pl.multiple_of(r * 16, 16), 16)
                    for h in (0, 1):
                        for t in (0, 1):
                            val = s.total(h, t, at)
                            if k == 0:
                                g[2 * h + t, y, 0, self.here(at), :] = val
                            else:
                                g[x, 2 * h + t, 1, self.here(at), :] = val

        def end_two(self):
            for k, s in enumerate(self.two):
                s.arrive()

                @pl.loop(0, RP // 32)
                def _(r):
                    at = pl.ds(pl.multiple_of(r * 16, 16), 16)
                    for h in (0, 1):
                        g[x, y, k, self.here(at, RP // 2 * h), :] = s.total(h, 0, at)

            rows = pl.ds(self.p * RP, RP)
            start(g.at[x, y, 1 - zl, rows], zbuf.at[self.p], self.base + 48, dev_zl)

        def out(self):
            rows = pl.ds(self.p * RP, RP)
            rdma(g.at[x, y, 1 - zl, rows], zbuf.at[self.p], self.base + 48, dev_zl).wait_recv()
            obuf[self.p] = (g[x, y, zl, rows] + zbuf[self.p]).astype(BF16)
            src, dst = obuf.at[self.p], obuf_in.at[self.p]

            @pl.when(is_self)
            def _():
                pltpu.make_async_copy(src, dst, lsem.at[2 + self.p]).start()

            @pl.when(jnp.logical_not(is_self))
            def _():
                rdma(src, dst, self.base + 49, owner).start()

        def done(self):
            src, dst = obuf.at[self.p], obuf_in.at[self.p]

            @pl.when(is_self)
            def _():
                pltpu.make_async_copy(src, dst, lsem.at[2 + self.p]).wait()

            @pl.when(jnp.logical_not(is_self))
            def _():
                rdma(src, dst, self.base + 49, owner).wait()

            grad_out[self.p * RP : (self.p + 1) * RP, :] = obuf_in[self.p]

    ga, gb = Gather(0), Gather(1)
    ea, eb = Collect(0), Collect(1)
    softmax(0)
    gradient(0)
    ga.begin()
    softmax(1)
    ga.backward(0)
    gradient(1)
    ga.near()
    gb.begin()
    ga.backward(3)
    ga.backward(1)
    ga.far()
    ga.backward(2)
    ea.begin(ea.one)
    gb.backward(0)
    ea.relay(ea.one)
    gb.near()
    ea.end_one()
    ea.begin(ea.two)
    gb.backward(3)
    ea.relay(ea.two)
    gb.backward(1)
    gb.far()
    ea.end_two()
    gb.backward(2)
    eb.begin(eb.one)
    ea.out()
    eb.relay(eb.one)
    eb.end_one()
    eb.begin(eb.two)
    eb.relay(eb.two)
    eb.end_two()
    eb.out()
    ea.done()
    eb.done()

    for cp in kit.pending:
        cp.wait_send()

    for p in range(NP):

        @pl.loop(1, NV)
        def _(r):
            peer_copy(p, r).wait_send()


NSEM = 34 + 4 * NP + 12 * NP + 9 * NP + 50 * NP


def body(hidden, head, targets, loss_weight):
    tile = (ROWS, WIDTH)
    vmem = pl.BlockSpec(memory_space=pltpu.VMEM)
    loss, grad = pl.pallas_call(
        kernel,
        out_shape=(
            jax.ShapeDtypeStruct((2, ROWS // 2), F32),
            jax.ShapeDtypeStruct(tile, BF16),
        ),
        in_specs=[vmem, pl.BlockSpec(memory_space=pl.ANY), vmem, vmem],
        out_specs=(vmem, vmem),
        scratch_shapes=[
            pltpu.VMEM((RING, RING, 2, *tile), BF16),
            pltpu.VMEM((SLAB, VL), BF16),
            pltpu.VMEM((RING, 2, NP, 2, RP, HV), F32),
            pltpu.VMEM((RING, NP, 2, RP, HV), F32),
            pltpu.VMEM((NP, 2, 6, 1, RP, HV), I16),
            pltpu.VMEM((NP, 2, RP, HV), F32),
            pltpu.VMEM((ROWS, 128), F32),
            pltpu.VMEM((ROWS, 1), jnp.int32),
            pltpu.VMEM((ROWS, 1), F32),
            pltpu.VMEM((ROWS, 128), F32),
            pltpu.VMEM((NP, 8, ROWS), F32),
            pltpu.VMEM((NP, NV - 1, 8, ROWS), F32),
            pltpu.VMEM((RING, 2, ROWS, VL), BF16),
            pltpu.VMEM((RING, RING, 2, *tile), F32),
            pltpu.VMEM((NP, 2, 2, 6, 2, RP, WIDTH), I16),
            pltpu.VMEM((NP, 2, 2, 6, 1, RP // 2, WIDTH), I16),
            pltpu.VMEM((NP, 5, 2, 6, 8, 128), F32),
            pltpu.VMEM((3, 6, 128, 128), F32),
            pltpu.VMEM((NP, RP, WIDTH), F32),
            pltpu.VMEM((NP, RP, WIDTH), BF16),
            pltpu.VMEM((NP, RP, WIDTH), BF16),
            pltpu.SemaphoreType.DMA((NSEM,)),
            pltpu.SemaphoreType.DMA((NSEM,)),
            pltpu.SemaphoreType.DMA((NP, NV - 1)),
            pltpu.SemaphoreType.DMA((NP, NV - 1)),
            pltpu.SemaphoreType.DMA((2 + NP,)),
        ],
        compiler_params=pltpu.CompilerParams(
            collective_id=0, has_side_effects=True, vmem_limit_bytes=60 * 1024 * 1024
        ),
        name="mtp_loss",
    )(hidden.reshape(tile), head, targets.T, loss_weight.T)
    rows, depths = targets.shape
    return loss.T, grad.reshape(rows, depths, WIDTH)


def solution(mesh):
    return jax.shard_map(
        body,
        mesh=mesh,
        in_specs=(P("ctx", None, "vocab"), P("ctx", "vocab"), P("ctx", None), P("ctx", None)),
        out_specs=(P("ctx", None), P("ctx", None, "vocab")),
        check_vma=False,
    )
```

```python
import jax
import jax.numpy as jnp
from jax import lax
from jax.experimental import pallas as pl
from jax.experimental.pallas import tpu as pltpu
from jax.sharding import PartitionSpec as P

F32 = jnp.float32
BF16 = jnp.bfloat16
RING = 4
NV = 32
ROWS = 128
WIDTH = 224
VL = 2048
HV = VL // 2
SLAB = 4 * WIDTH
NP = 2
RP = ROWS // NP
I16 = jnp.int16
LEVELS = 32766.0
HOPS = ((2, 0, 0), (2, 1, 1), (3, 1, 0), (1, 0, 1), (3, 0, 0), (1, 1, 1))


class Ring4Sum:
    def __init__(self, k, base, value, tiles, rows, block, coded, sides, plus, minus):
        self.k, self.base, self.value = k, base, value
        self.tiles, self.rows, self.block = tiles, rows, block
        (self.out, self.land), (self.sout, self.sland, self.cols) = coded, sides
        self.plus, self.minus = plus, minus

    def copies(self, i):
        dev = self.plus if HOPS[i][2] else self.minus
        b = self.base + 2 * i
        return (
            self.k.rdma(self.out.at[i], self.land.at[i], b, dev),
            self.k.rdma(self.sout.at[i], self.sland.at[i], b + 1, dev),
        )

    def send(self, i, landed=()):
        d, h, _ = HOPS[i]
        stat = self.k.stat
        lanes = lax.broadcasted_iota(jnp.int32, (self.block, 128), 1)

        for r in range(self.rows // self.block):
            at = pl.ds(r * self.block, self.block)
            side = jnp.zeros((self.block, 128), F32)
            for t in range(self.tiles):
                val = self.value(d, h, t, at)
                for j in landed:
                    val = val + self.decoded(j, t, at)
                low = jnp.min(val, axis=1, keepdims=True)
                high = jnp.max(val, axis=1, keepdims=True)
                middle = 0.5 * low + 0.5 * high
                span = jnp.maximum(0.5 * high - 0.5 * low, 1e-30)
                steps = jnp.clip(jnp.round((val - middle) * (LEVELS / span)), -LEVELS, LEVELS)
                self.out[i, t, at, :] = steps.astype(jnp.int32).astype(I16)
                side = jnp.where(lanes == 2 * t, middle, side)
                side = jnp.where(lanes == 2 * t + 1, span * (1.0 / LEVELS), side)
            stat[at, :] = side

        self.sout[i] = jnp.transpose(stat[...])[:8]
        for cp in self.copies(i):
            cp.start()
            self.k.pending.append(cp)

    def receive(self, i):
        for cp in self.copies(i):
            cp.wait_recv()
        rows = jnp.concatenate([self.sland[i]] * 16, axis=0)
        self.cols[i] = jnp.transpose(rows)

    def decoded(self, i, t, at):
        steps = self.land[i, t, at, :].astype(jnp.int32).astype(F32)
        return steps * self.cols[i, at, 2 * t + 1 : 2 * t + 2] + self.cols[i, at, 2 * t : 2 * t + 1]

    def relay(self):
        self.receive(0)
        self.send(4, (0,))
        self.receive(1)
        self.send(5, (1,))

    def arrive(self):
        for i in (2, 3, 4, 5):
            self.receive(i)

    def total(self, h, t, at):
        i, j = ((3, 4), (2, 5))[h]
        return self.value(0, h, t, at) + self.decoded(i, t, at) + self.decoded(j, t, at)


class Tools:
    def __init__(self, ssem, rsem, stat):
        self.ssem, self.rsem, self.stat, self.pending = ssem, rsem, stat, []

    def rdma(self, src, dst, i, dev):
        return pltpu.make_async_remote_copy(
            src_ref=src,
            dst_ref=dst,
            send_sem=self.ssem.at[i],
            recv_sem=self.rsem.at[i],
            device_id=dev,
            device_id_type=pl.DeviceIdType.MESH,
        )

    def start(self, src, dst, i, dev):
        cp = self.rdma(src, dst, i, dev)
        cp.start()
        self.pending.append(cp)


def kernel(
    hid,
    head_hbm,
    tgt,
    wgt,
    loss_out,
    grad_out,
    buf,
    head,
    part,
    pair,
    zcode,
    logit,
    stat,
    tcol,
    wcol,
    lcol,
    msg,
    peers,
    dl,
    g,
    code1,
    code2,
    sides,
    cols,
    zbuf,
    obuf,
    obuf_in,
    ssem,
    rsem,
    st_s,
    st_r,
    lsem,
):
    c = lax.axis_index("ctx")
    v = lax.axis_index("vocab")
    zh, core = c // 2, c % 2
    x, y, zl = v // 8, (v // 2) % 4, v % 2
    kit = Tools(ssem, rsem, stat)
    rdma, start = kit.rdma, kit.start

    def up(i, d):
        return (i + d) % RING

    def dev_zh(d):
        return (up(zh, d) * 2 + core, v)

    def dev_x(d):
        return (c, up(x, d) * 8 + y * 2 + zl)

    def dev_y(d):
        return (c, x * 8 + up(y, d) * 2 + zl)

    partner = (zh * 2 + 1 - core, v)
    dev_zl = (c, x * 8 + y * 2 + 1 - zl)
    hx, hy = up(x, zh), core * 2 + y % 2
    holder = (v // 4, hx * 8 + hy * 2 + zl)
    owner = (up(x, 4 - zh) * 2 + y // 2, 4 * c + v % 4)
    is_self = jnp.logical_and(holder[0] == c, holder[1] == v)

    head_copy = pltpu.make_async_copy(head_hbm, head, lsem.at[0])
    head_copy.start()

    barrier = pltpu.get_barrier_semaphore()

    def greet(dev):
        pl.semaphore_signal(barrier, inc=1, device_id=dev, device_id_type=pl.DeviceIdType.MESH)

    for dev in (
        partner,
        dev_zh(1),
        dev_zh(3),
        dev_x(1),
        dev_x(3),
        dev_y(1),
        dev_y(3),
        dev_zl,
    ):
        greet(dev)

    @pl.when(jnp.logical_not(is_self))
    def _():
        greet(holder)
        greet(owner)
        pl.semaphore_wait(barrier, 10)

    @pl.when(is_self)
    def _():
        pl.semaphore_wait(barrier, 8)

    @pl.when(is_self)
    def _():
        cp = pltpu.make_async_copy(hid, buf.at[x, y, zl], lsem.at[1])
        cp.start()
        cp.wait()

    @pl.when(jnp.logical_not(is_self))
    def _():
        cp = rdma(hid, buf.at[hx, hy, zl], 0, holder)
        cp.start()
        cp.wait_send()
        rdma(hid, buf.at[x, y, zl], 0, holder).wait_recv()

    start(buf.at[x, y, zl], buf.at[x, y, zl], 1, dev_zl)

    row = lax.broadcasted_iota(jnp.int32, (ROWS, ROWS // 2), 0)
    tok = lax.broadcasted_iota(jnp.int32, (ROWS, ROWS // 2), 1)

    def as_column(pairs):
        both = jnp.where(row % 2 == 1, pairs[1:2, :], pairs[0:1, :])
        return jnp.sum(jnp.where(row // 2 == tok, both, 0.0), axis=1, keepdims=True)

    tcol[...] = as_column(tgt[...].astype(F32)).astype(jnp.int32)
    wcol[...] = as_column(wgt[...])

    rdma(buf.at[x, y, zl], buf.at[x, y, 1 - zl], 1, dev_zl).wait_recv()

    lines = (
        (lambda a, b: buf.at[a, b, 0], x, y, dev_x, dev_y),
        (lambda a, b: buf.at[b, a, 1], y, x, dev_y, dev_x),
    )
    for k, (at, a, b, dev_a, dev_b) in enumerate(lines):
        base = 2 + 16 * k
        for d in (1, 3):
            start(at(a, b), at(a, b), base + (0 if d == 1 else 1), dev_a(d))
    steps = (0, 3, 1, 2)

    def second(k, n):
        at, a, b, dev_a, dev_b = lines[k]
        base = 2 + 16 * k
        for d, o in ((1, 4), (3, 8)):
            tile = at(up(a, steps[n]), b)
            start(tile, tile, base + o + n, dev_b(d))

    def second_in(k, n, d):
        at, a, b, dev_a, dev_b = lines[k]
        base = 2 + 16 * k
        tile = at(up(a, steps[n]), up(b, 4 - d))
        rdma(tile, tile, base + (4 if d == 1 else 8) + n, dev_b(d)).wait_recv()
        return tile

    for k in (0, 1):
        second(k, 0)
    for k, (at, a, b, dev_a, dev_b) in enumerate(lines):
        base = 2 + 16 * k
        for d, i, rows in ((1, 0, pl.ds(0, 64)), (3, 1, pl.ds(64, 64))):
            tile = at(up(a, 4 - d), b)
            rdma(tile, tile, base + i, dev_a(d)).wait_recv()
            half = tile.at[rows]
            start(half, half, base + 2 + i, dev_a(d))
            second(k, 1 + i)
    for k, (at, a, b, dev_a, dev_b) in enumerate(lines):
        base = 2 + 16 * k
        for d, i, rows in ((1, 0, pl.ds(0, 64)), (3, 1, pl.ds(64, 64))):
            half = at(up(a, 2), b).at[rows]
            rdma(half, half, base + 2 + i, dev_a(d)).wait_recv()
        second(k, 3)
    for n, d in ((0, 1), (1, 1), (2, 3), (3, 3)):
        for k, (at, a, b, dev_a, dev_b) in enumerate(lines):
            tile = second_in(k, n, d)
            start(tile, tile, 2 + 16 * k + 12 + n, dev_b(d))
    for k, (at, a, b, dev_a, dev_b) in enumerate(lines):
        for n, d in ((2, 1), (3, 1), (0, 3), (1, 3)):
            second_in(k, n, d)
        for n in range(4):
            tile = at(up(a, steps[n]), up(b, 2))
            rdma(tile, tile, 2 + 16 * k + 12 + n, dev_b(1)).wait_recv()
    sem = 34

    head_copy.wait()

    def forward(d, h):
        q = up(zh, d)
        at = up(q, zh)

        @pl.loop(0, HV // 256)
        def _(n):
            cs = pl.ds(pl.multiple_of(h * HV + n * 256, 256), 256)
            out_cs = pl.ds(pl.multiple_of(n * 256, 256), 256)
            acc = None
            for j in range(4):
                lhs = jnp.concatenate([buf[at, j // 2, j % 2], buf[at, 2 + j // 2, j % 2]], axis=0)
                term = jnp.dot(
                    lhs, head[j * WIDTH : (j + 1) * WIDTH, cs], preferred_element_type=F32
                )
                acc = term if acc is None else acc + term
            for k in range(2):
                for p in range(NP):
                    lo = k * ROWS + p * RP
                    part[q, k, p, h, :, out_cs] = acc[lo : lo + RP]

        for p in range(NP):
            start(part.at[q, 1 - core, p, h], pair.at[q, p, h], pair_sem(d, p, h), partner)

    def pair_sem(d, p, h):
        return sem + (d * NP + p) * 2 + h

    def pair_in(d, p, h):
        q = up(zh, d)
        rdma(part.at[q, 1 - core, p, h], pair.at[q, p, h], pair_sem(d, p, h), partner).wait_recv()

    zr = [
        Ring4Sum(
            kit,
            sem + 8 * NP + 12 * p,
            lambda d, h, t, at, p=p: part[up(zh, d), core, p, h, at, :]
            + pair[up(zh, d), p, h, at, :],
            1,
            RP,
            16,
            (zcode.at[p, 0], zcode.at[p, 1]),
            (sides.at[p, 0, 0], sides.at[p, 0, 1], cols.at[0]),
            dev_zh(1),
            dev_zh(3),
        )
        for p in range(NP)
    ]
    def logits_begin(p):
        for h in (0, 1):
            pair_in(2, p, h)
            zr[p].send(h)

    forward(2, 0)
    forward(2, 1)
    logits_begin(0)
    forward(3, 1)
    pair_in(3, 0, 1)
    zr[0].send(2)
    forward(1, 0)
    pair_in(1, 0, 0)
    zr[0].send(3)
    forward(3, 0)
    forward(1, 1)
    pair_in(3, 0, 0)
    pair_in(1, 0, 1)
    zr[0].relay()
    logits_begin(1)
    pair_in(3, 1, 1)
    zr[1].send(2)
    pair_in(1, 1, 0)
    zr[1].send(3)
    forward(0, 0)
    forward(0, 1)
    pair_in(3, 1, 0)
    pair_in(1, 1, 1)
    sem2 = sem + 8 * NP + 12 * NP

    lanes = lax.broadcasted_iota(jnp.int32, (16, 128), 1)
    cols0 = lax.broadcasted_iota(jnp.int32, (16, HV), 1) + v * VL

    def peer_copy(p, r):
        return pltpu.make_async_remote_copy(
            src_ref=msg.at[p],
            dst_ref=peers.at[p, r - 1],
            send_sem=st_s.at[p, r - 1],
            recv_sem=st_r.at[p, r - 1],
            device_id=(c, (v + r) % NV),
            device_id_type=pl.DeviceIdType.MESH,
        )

    def softmax(p):
        for h in (0, 1):
            pair_in(0, p, h)
        zr[p].arrive()

        @pl.loop(0, RP // 16)
        def _(r):
            at = pl.ds(pl.multiple_of(r * 16, 16), 16)
            t = tcol[pl.ds(pl.multiple_of(p * RP + r * 16, 16), 16), :]
            l0 = zr[p].total(0, 0, at)
            l1 = zr[p].total(1, 0, at)
            top = jnp.maximum(
                jnp.max(l0, axis=1, keepdims=True), jnp.max(l1, axis=1, keepdims=True)
            )
            hit = jnp.sum(jnp.where(cols0 == t, l0, 0.0), axis=1, keepdims=True) + jnp.sum(
                jnp.where(cols0 + HV == t, l1, 0.0), axis=1, keepdims=True
            )
            e0 = jnp.exp(l0 - top)
            e1 = jnp.exp(l1 - top)
            total = jnp.sum(e0, axis=1, keepdims=True) + jnp.sum(e1, axis=1, keepdims=True)
            logit[p, 0, at, :] = e0
            logit[p, 1, at, :] = e1
            stat[at, :] = jnp.where(lanes == 0, top, jnp.where(lanes == 1, total, hit))

        msg[p] = jnp.transpose(stat[...])[:8]

        @pl.loop(1, NV)
        def _(r):
            peer_copy(p, r).start()

    def gradient(p):
        @pl.loop(1, NV)
        def _(r):
            peer_copy(p, r).wait_recv()

        top, total, hit = msg[p, 0:1, :], msg[p, 1:2, :], msg[p, 2:3, :]
        tops = peers[p, :, 0, :]
        best = jnp.maximum(top, jnp.max(tops, axis=0, keepdims=True))
        everyone = total * jnp.exp(top - best) + jnp.sum(
            peers[p, :, 1, :] * jnp.exp(tops - best), axis=0, keepdims=True
        )
        hits = hit + jnp.sum(peers[p, :, 2, :], axis=0, keepdims=True)
        loss = jnp.log(everyone) + best - hits
        scale = jnp.exp(top - best) / everyone
        odd = lax.broadcasted_iota(jnp.int32, (128, 128), 0) % 2 == 1
        lcol[...] = jnp.transpose(jnp.where(odd, loss, scale))
        spot = lax.broadcasted_iota(jnp.int32, (RP, ROWS // 2), 1) * 2
        line = lax.broadcasted_iota(jnp.int32, (RP, ROWS // 2), 0) + p * RP
        for d in (0, 1):
            found = jnp.sum(
                jnp.where(line == spot + d, lcol[:RP, 1:2], 0.0), axis=0, keepdims=True
            )
            loss_out[d : d + 1, :] = found if p == 0 else loss_out[d : d + 1, :] + found

        @pl.loop(0, RP // 16)
        def _(r):
            at = pl.ds(pl.multiple_of(r * 16, 16), 16)
            here = pl.ds(pl.multiple_of(p * RP + r * 16, 16), 16)
            t = tcol[here, :]
            w = wcol[here, :]
            s = lcol[at, 0:1]
            for h in (0, 1):
                one = (cols0 + h * HV == t).astype(F32)
                dl[zh, core, here, h * HV : (h + 1) * HV] = (
                    w * (logit[p, h, at, :] * s - one)
                ).astype(BF16)

    class Gather:
        def __init__(self, p):
            self.p, self.base = p, sem2 + 9 * p
            self.all = pl.ds(p * RP, RP)
            self.first = pl.ds(p * RP, RP // 2)
            self.last = pl.ds(p * RP + RP // 2, RP // 2)

        def go(self, d, k, rows, i, dev):
            slot = dl.at[up(zh, d), k, rows]
            start(slot, slot, self.base + i, dev)

        def come(self, d, k, rows, i):
            slot = dl.at[up(zh, d), k, rows]
            rdma(slot, slot, self.base + i, partner).wait_recv()

        def begin(self):
            self.go(0, core, self.all, 0, dev_zh(1))
            self.go(0, core, self.all, 1, dev_zh(3))
            self.go(0, core, self.all, 2, partner)

        def near(self):
            self.come(3, core, self.all, 0)
            self.go(3, core, self.first, 3, dev_zh(1))
            self.come(1, core, self.all, 1)
            self.go(1, core, self.last, 5, dev_zh(3))
            self.go(3, core, self.all, 4, partner)
            self.go(1, core, self.all, 6, partner)

        def far(self):
            self.come(2, core, self.first, 3)
            self.go(2, core, self.first, 7, partner)
            self.come(2, core, self.last, 5)
            self.go(2, core, self.last, 8, partner)

        def backward(self, *ds):
            other = 1 - core
            for d in ds:
                if d == 2:
                    self.come(2, other, self.first, 7)
                    self.come(2, other, self.last, 8)
                else:
                    self.come(d, other, self.all, {0: 2, 3: 4, 1: 6}[d])
            lhs = [dl[up(zh, d), k, self.all] for d in ds for k in (0, 1)]
            lhs = jnp.concatenate(lhs, axis=0)
            for j in range(4):
                res = lax.dot_general(
                    lhs,
                    head[j * WIDTH : (j + 1) * WIDTH, :],
                    (((1,), (1,)), ((), ())),
                    preferred_element_type=F32,
                )
                for i, d in enumerate(ds):
                    at = up(up(zh, d), zh)
                    for k in (0, 1):
                        lo = (2 * i + k) * RP
                        g[at, 2 * k + j // 2, j % 2, self.all] = res[lo : lo + RP]

    class Collect:
        def __init__(self, p):
            self.p = p
            base = sem2 + 9 * NP + (48 + 2) * p
            self.base = base

            def here(at, lo=0):
                return pl.ds(p * RP + lo + at.start, at.size)

            self.here = here

            def ring(i, k, value, tiles, rows, code, dev):
                return Ring4Sum(
                    kit,
                    base + 12 * i,
                    value,
                    tiles,
                    rows,
                    rows,
                    (code.at[p, k, 0], code.at[p, k, 1]),
                    (sides.at[p, 1 + i, 0], sides.at[p, 1 + i, 1], cols.at[1 + k]),
                    dev(1),
                    dev(3),
                )

            self.one = (
                ring(0, 0, lambda d, h, t, at: g[2 * h + t, up(y, d), 0, here(at), :], 2, RP, code1, dev_y),
                ring(1, 1, lambda d, h, t, at: g[up(x, d), 2 * h + t, 1, here(at), :], 2, RP, code1, dev_x),
            )
            half = RP // 2
            self.two = (
                ring(2, 0, lambda d, h, t, at: g[up(x, d), y, 0, here(at, half * h), :], 1, half, code2, dev_x),
                ring(3, 1, lambda d, h, t, at: g[x, up(y, d), 1, here(at, half * h), :], 1, half, code2, dev_y),
            )

        def begin(self, stage):
            for i in (0, 1, 2, 3):
                for s in stage:
                    s.send(i)

        def relay(self, stage):
            for s in stage:
                s.relay()

        def end_one(self):
            for k, s in enumerate(self.one):
                s.arrive()

                at = pl.ds(0, RP)
                for h in (0, 1):
                    for t in (0, 1):
                        val = s.total(h, t, at)
                        if k == 0:
                            g[2 * h + t, y, 0, self.here(at), :] = val
                        else:
                            g[x, 2 * h + t, 1, self.here(at), :] = val

        def end_two(self):
            for k, s in enumerate(self.two):
                s.arrive()

                at = pl.ds(0, RP // 2)
                for h in (0, 1):
                    g[x, y, k, self.here(at, RP // 2 * h), :] = s.total(h, 0, at)

            rows = pl.ds(self.p * RP, RP)
            start(g.at[x, y, 1 - zl, rows], zbuf.at[self.p], self.base + 48, dev_zl)

        def out(self):
            rows = pl.ds(self.p * RP, RP)
            rdma(g.at[x, y, 1 - zl, rows], zbuf.at[self.p], self.base + 48, dev_zl).wait_recv()
            obuf[self.p] = (g[x, y, zl, rows] + zbuf[self.p]).astype(BF16)
            src, dst = obuf.at[self.p], obuf_in.at[self.p]

            @pl.when(is_self)
            def _():
                pltpu.make_async_copy(src, dst, lsem.at[2 + self.p]).start()

            @pl.when(jnp.logical_not(is_self))
            def _():
                rdma(src, dst, self.base + 49, owner).start()

        def done(self):
            src, dst = obuf.at[self.p], obuf_in.at[self.p]

            @pl.when(is_self)
            def _():
                pltpu.make_async_copy(src, dst, lsem.at[2 + self.p]).wait()

            @pl.when(jnp.logical_not(is_self))
            def _():
                rdma(src, dst, self.base + 49, owner).wait()

            grad_out[self.p * RP : (self.p + 1) * RP, :] = obuf_in[self.p]

    ga, gb = Gather(0), Gather(1)
    ea, eb = Collect(0), Collect(1)
    softmax(0)
    zr[1].relay()
    gradient(0)
    ga.begin()
    softmax(1)
    ga.backward(0)
    gradient(1)
    ga.near()
    gb.begin()
    ga.backward(3, 1)
    ga.far()
    ga.backward(2)
    ea.begin(ea.one)
    gb.backward(0)
    ea.relay(ea.one)
    gb.near()
    ea.end_one()
    ea.begin(ea.two)
    gb.backward(3, 1)
    gb.far()
    ea.relay(ea.two)
    gb.backward(2)
    eb.begin(eb.one)
    ea.end_two()
    eb.relay(eb.one)
    ea.out()
    eb.end_one()
    eb.begin(eb.two)
    eb.relay(eb.two)
    eb.end_two()
    eb.out()
    ea.done()
    eb.done()

    for cp in kit.pending:
        cp.wait_send()

    for p in range(NP):

        @pl.loop(1, NV)
        def _(r):
            peer_copy(p, r).wait_send()


NSEM = 34 + 8 * NP + 12 * NP + 9 * NP + 50 * NP


def body(hidden, head, targets, loss_weight):
    tile = (ROWS, WIDTH)
    vmem = pl.BlockSpec(memory_space=pltpu.VMEM)
    loss, grad = pl.pallas_call(
        kernel,
        out_shape=(
            jax.ShapeDtypeStruct((2, ROWS // 2), F32),
            jax.ShapeDtypeStruct(tile, BF16),
        ),
        in_specs=[vmem, pl.BlockSpec(memory_space=pl.ANY), vmem, vmem],
        out_specs=(vmem, vmem),
        scratch_shapes=[
            pltpu.VMEM((RING, RING, 2, *tile), BF16),
            pltpu.VMEM((SLAB, VL), BF16),
            pltpu.VMEM((RING, 2, NP, 2, RP, HV), F32),
            pltpu.VMEM((RING, NP, 2, RP, HV), F32),
            pltpu.VMEM((NP, 2, 6, 1, RP, HV), I16),
            pltpu.VMEM((NP, 2, RP, HV), F32),
            pltpu.VMEM((ROWS, 128), F32),
            pltpu.VMEM((ROWS, 1), jnp.int32),
            pltpu.VMEM((ROWS, 1), F32),
            pltpu.VMEM((ROWS, 128), F32),
            pltpu.VMEM((NP, 8, ROWS), F32),
            pltpu.VMEM((NP, NV - 1, 8, ROWS), F32),
            pltpu.VMEM((RING, 2, ROWS, VL), BF16),
            pltpu.VMEM((RING, RING, 2, *tile), F32),
            pltpu.VMEM((NP, 2, 2, 6, 2, RP, WIDTH), I16),
            pltpu.VMEM((NP, 2, 2, 6, 1, RP // 2, WIDTH), I16),
            pltpu.VMEM((NP, 5, 2, 6, 8, 128), F32),
            pltpu.VMEM((3, 6, 128, 128), F32),
            pltpu.VMEM((NP, RP, WIDTH), F32),
            pltpu.VMEM((NP, RP, WIDTH), BF16),
            pltpu.VMEM((NP, RP, WIDTH), BF16),
            pltpu.SemaphoreType.DMA((NSEM,)),
            pltpu.SemaphoreType.DMA((NSEM,)),
            pltpu.SemaphoreType.DMA((NP, NV - 1)),
            pltpu.SemaphoreType.DMA((NP, NV - 1)),
            pltpu.SemaphoreType.DMA((2 + NP,)),
        ],
        compiler_params=pltpu.CompilerParams(
            collective_id=0, has_side_effects=True, vmem_limit_bytes=60 * 1024 * 1024
        ),
        name="mtp_loss",
    )(hidden.reshape(tile), head, targets.T, loss_weight.T)
    rows, depths = targets.shape
    return loss.T, grad.reshape(rows, depths, WIDTH)


def solution(mesh):
    return jax.shard_map(
        body,
        mesh=mesh,
        in_specs=(P("ctx", None, "vocab"), P("ctx", "vocab"), P("ctx", None), P("ctx", None)),
        out_specs=(P("ctx", None), P("ctx", None, "vocab")),
        check_vma=False,
    )
```

```python
import jax
import jax.numpy as jnp
from jax import lax
from jax.experimental import pallas as pl
from jax.experimental.pallas import tpu as pltpu
from jax.sharding import PartitionSpec as P

F32 = jnp.float32
BF16 = jnp.bfloat16
RING = 4
NV = 32
ROWS = 128
WIDTH = 224
VL = 2048
HV = VL // 2
SLAB = 4 * WIDTH
NP = 2
RP = ROWS // NP
I16 = jnp.int16
LEVELS = 32766.0
HOPS = ((2, 0, 0), (2, 1, 1), (3, 1, 0), (1, 0, 1), (3, 0, 0), (1, 1, 1))


class Ring4Sum:
    def __init__(self, k, base, value, tiles, rows, block, coded, sides, plus, minus):
        self.k, self.base, self.value = k, base, value
        self.tiles, self.rows, self.block = tiles, rows, block
        (self.out, self.land), (self.sout, self.sland, self.cols) = coded, sides
        self.plus, self.minus = plus, minus

    def copies(self, i):
        dev = self.plus if HOPS[i][2] else self.minus
        b = self.base + 2 * i
        return (
            self.k.rdma(self.out.at[i], self.land.at[i], b, dev),
            self.k.rdma(self.sout.at[i], self.sland.at[i], b + 1, dev),
        )

    def send(self, i, landed=()):
        d, h, _ = HOPS[i]
        stat = self.k.stat
        lanes = lax.broadcasted_iota(jnp.int32, (self.block, 128), 1)

        for r in range(self.rows // self.block):
            at = pl.ds(r * self.block, self.block)
            side = jnp.zeros((self.block, 128), F32)
            for t in range(self.tiles):
                val = self.value(d, h, t, at)
                for j in landed:
                    val = val + self.decoded(j, t, at)
                low = jnp.min(val, axis=1, keepdims=True)
                high = jnp.max(val, axis=1, keepdims=True)
                middle = 0.5 * low + 0.5 * high
                span = jnp.maximum(0.5 * high - 0.5 * low, 1e-30)
                steps = jnp.clip(jnp.round((val - middle) * (LEVELS / span)), -LEVELS, LEVELS)
                self.out[i, t, at, :] = steps.astype(jnp.int32).astype(I16)
                side = jnp.where(lanes == 2 * t, middle, side)
                side = jnp.where(lanes == 2 * t + 1, span * (1.0 / LEVELS), side)
            stat[at, :] = side

        self.sout[i] = jnp.transpose(stat[...])[:8]
        for cp in self.copies(i):
            cp.start()
            self.k.pending.append(cp)

    def receive(self, i):
        for cp in self.copies(i):
            cp.wait_recv()
        rows = jnp.concatenate([self.sland[i]] * 16, axis=0)
        self.cols[i] = jnp.transpose(rows)

    def decoded(self, i, t, at):
        steps = self.land[i, t, at, :].astype(jnp.int32).astype(F32)
        return steps * self.cols[i, at, 2 * t + 1 : 2 * t + 2] + self.cols[i, at, 2 * t : 2 * t + 1]

    def relay(self):
        self.receive(0)
        self.send(4, (0,))
        self.receive(1)
        self.send(5, (1,))

    def arrive(self):
        for i in (2, 3, 4, 5):
            self.receive(i)

    def total(self, h, t, at):
        i, j = ((3, 4), (2, 5))[h]
        return self.value(0, h, t, at) + self.decoded(i, t, at) + self.decoded(j, t, at)


class Tools:
    def __init__(self, ssem, rsem, stat):
        self.ssem, self.rsem, self.stat, self.pending = ssem, rsem, stat, []

    def rdma(self, src, dst, i, dev):
        return pltpu.make_async_remote_copy(
            src_ref=src,
            dst_ref=dst,
            send_sem=self.ssem.at[i],
            recv_sem=self.rsem.at[i],
            device_id=dev,
            device_id_type=pl.DeviceIdType.MESH,
        )

    def start(self, src, dst, i, dev):
        cp = self.rdma(src, dst, i, dev)
        cp.start()
        self.pending.append(cp)


def kernel(
    hid,
    head_hbm,
    tgt,
    wgt,
    loss_out,
    grad_out,
    buf,
    head,
    part,
    pair,
    zcode,
    logit,
    stat,
    tcol,
    wcol,
    lcol,
    msg,
    peers,
    dl,
    g,
    code1,
    land2,
    sides,
    cols,
    zbuf,
    obuf,
    obuf_in,
    ssem,
    rsem,
    st_s,
    st_r,
    lsem,
):
    c = lax.axis_index("ctx")
    v = lax.axis_index("vocab")
    zh, core = c // 2, c % 2
    x, y, zl = v // 8, (v // 2) % 4, v % 2
    kit = Tools(ssem, rsem, stat)
    rdma, start = kit.rdma, kit.start

    def up(i, d):
        return (i + d) % RING

    def dev_zh(d):
        return (up(zh, d) * 2 + core, v)

    def dev_x(d):
        return (c, up(x, d) * 8 + y * 2 + zl)

    def dev_y(d):
        return (c, x * 8 + up(y, d) * 2 + zl)

    partner = (zh * 2 + 1 - core, v)
    dev_zl = (c, x * 8 + y * 2 + 1 - zl)
    hx, hy = up(x, zh), core * 2 + y % 2
    holder = (v // 4, hx * 8 + hy * 2 + zl)
    owner = (up(x, 4 - zh) * 2 + y // 2, 4 * c + v % 4)
    is_self = jnp.logical_and(holder[0] == c, holder[1] == v)

    head_copy = pltpu.make_async_copy(head_hbm, head, lsem.at[0])
    head_copy.start()

    barrier = pltpu.get_barrier_semaphore()

    def greet(dev):
        pl.semaphore_signal(barrier, inc=1, device_id=dev, device_id_type=pl.DeviceIdType.MESH)

    for dev in (
        partner,
        dev_zh(1),
        dev_zh(3),
        dev_x(1),
        dev_x(3),
        dev_y(1),
        dev_y(3),
        dev_zl,
    ):
        greet(dev)

    @pl.when(jnp.logical_not(is_self))
    def _():
        greet(holder)
        greet(owner)
        pl.semaphore_wait(barrier, 10)

    @pl.when(is_self)
    def _():
        pl.semaphore_wait(barrier, 8)

    @pl.when(is_self)
    def _():
        cp = pltpu.make_async_copy(hid, buf.at[x, y, zl], lsem.at[1])
        cp.start()
        cp.wait()

    @pl.when(jnp.logical_not(is_self))
    def _():
        cp = rdma(hid, buf.at[hx, hy, zl], 0, holder)
        cp.start()
        cp.wait_send()
        rdma(hid, buf.at[x, y, zl], 0, holder).wait_recv()

    start(buf.at[x, y, zl], buf.at[x, y, zl], 1, dev_zl)

    row = lax.broadcasted_iota(jnp.int32, (ROWS, ROWS // 2), 0)
    tok = lax.broadcasted_iota(jnp.int32, (ROWS, ROWS // 2), 1)

    def as_column(pairs):
        both = jnp.where(row % 2 == 1, pairs[1:2, :], pairs[0:1, :])
        return jnp.sum(jnp.where(row // 2 == tok, both, 0.0), axis=1, keepdims=True)

    tcol[...] = as_column(tgt[...].astype(F32)).astype(jnp.int32)
    wcol[...] = as_column(wgt[...])

    rdma(buf.at[x, y, zl], buf.at[x, y, 1 - zl], 1, dev_zl).wait_recv()

    lines = (
        (lambda a, b: buf.at[a, b, 0], x, y, dev_x, dev_y),
        (lambda a, b: buf.at[b, a, 1], y, x, dev_y, dev_x),
    )
    for k, (at, a, b, dev_a, dev_b) in enumerate(lines):
        base = 2 + 16 * k
        for d in (1, 3):
            start(at(a, b), at(a, b), base + (0 if d == 1 else 1), dev_a(d))
    steps = (0, 3, 1, 2)

    def second(k, n):
        at, a, b, dev_a, dev_b = lines[k]
        base = 2 + 16 * k
        for d, o in ((1, 4), (3, 8)):
            tile = at(up(a, steps[n]), b)
            start(tile, tile, base + o + n, dev_b(d))

    def second_in(k, n, d):
        at, a, b, dev_a, dev_b = lines[k]
        base = 2 + 16 * k
        tile = at(up(a, steps[n]), up(b, 4 - d))
        rdma(tile, tile, base + (4 if d == 1 else 8) + n, dev_b(d)).wait_recv()
        return tile

    for k in (0, 1):
        second(k, 0)
    for k, (at, a, b, dev_a, dev_b) in enumerate(lines):
        base = 2 + 16 * k
        for d, i, rows in ((1, 0, pl.ds(0, 64)), (3, 1, pl.ds(64, 64))):
            tile = at(up(a, 4 - d), b)
            rdma(tile, tile, base + i, dev_a(d)).wait_recv()
            half = tile.at[rows]
            start(half, half, base + 2 + i, dev_a(d))
            second(k, 1 + i)
    for k, (at, a, b, dev_a, dev_b) in enumerate(lines):
        base = 2 + 16 * k
        for d, i, rows in ((1, 0, pl.ds(0, 64)), (3, 1, pl.ds(64, 64))):
            half = at(up(a, 2), b).at[rows]
            rdma(half, half, base + 2 + i, dev_a(d)).wait_recv()
        second(k, 3)
    for n, d in ((0, 1), (1, 1), (2, 3), (3, 3)):
        for k, (at, a, b, dev_a, dev_b) in enumerate(lines):
            tile = second_in(k, n, d)
            start(tile, tile, 2 + 16 * k + 12 + n, dev_b(d))
    for k, (at, a, b, dev_a, dev_b) in enumerate(lines):
        for n, d in ((2, 1), (3, 1), (0, 3), (1, 3)):
            second_in(k, n, d)
        for n in range(4):
            tile = at(up(a, steps[n]), up(b, 2))
            rdma(tile, tile, 2 + 16 * k + 12 + n, dev_b(1)).wait_recv()
    sem = 34

    head_copy.wait()

    def forward(d, h):
        q = up(zh, d)
        at = up(q, zh)

        @pl.loop(0, HV // 256)
        def _(n):
            cs = pl.ds(pl.multiple_of(h * HV + n * 256, 256), 256)
            out_cs = pl.ds(pl.multiple_of(n * 256, 256), 256)
            acc = None
            for j in range(4):
                lhs = jnp.concatenate([buf[at, j // 2, j % 2], buf[at, 2 + j // 2, j % 2]], axis=0)
                term = jnp.dot(
                    lhs, head[j * WIDTH : (j + 1) * WIDTH, cs], preferred_element_type=F32
                )
                acc = term if acc is None else acc + term
            for k in range(2):
                for p in range(NP):
                    lo = k * ROWS + p * RP
                    part[q, k, p, h, :, out_cs] = acc[lo : lo + RP]

        for p in range(NP):
            start(part.at[q, 1 - core, p, h], pair.at[q, p, h], pair_sem(d, p, h), partner)

    def pair_sem(d, p, h):
        return sem + (d * NP + p) * 2 + h

    def pair_in(d, p, h):
        q = up(zh, d)
        rdma(part.at[q, 1 - core, p, h], pair.at[q, p, h], pair_sem(d, p, h), partner).wait_recv()

    zr = [
        Ring4Sum(
            kit,
            sem + 8 * NP + 12 * p,
            lambda d, h, t, at, p=p: part[up(zh, d), core, p, h, at, :]
            + pair[up(zh, d), p, h, at, :],
            1,
            RP,
            16,
            (zcode.at[p, 0], zcode.at[p, 1]),
            (sides.at[p, 0, 0], sides.at[p, 0, 1], cols.at[0]),
            dev_zh(1),
            dev_zh(3),
        )
        for p in range(NP)
    ]
    def logits_begin(p):
        for h in (0, 1):
            pair_in(2, p, h)
            zr[p].send(h)

    forward(2, 0)
    forward(2, 1)
    logits_begin(0)
    forward(3, 1)
    pair_in(3, 0, 1)
    zr[0].send(2)
    forward(1, 0)
    pair_in(1, 0, 0)
    zr[0].send(3)
    forward(3, 0)
    forward(1, 1)
    pair_in(3, 0, 0)
    pair_in(1, 0, 1)
    zr[0].relay()
    logits_begin(1)
    pair_in(3, 1, 1)
    zr[1].send(2)
    pair_in(1, 1, 0)
    zr[1].send(3)
    forward(0, 0)
    forward(0, 1)
    pair_in(3, 1, 0)
    pair_in(1, 1, 1)
    sem2 = sem + 8 * NP + 12 * NP

    lanes = lax.broadcasted_iota(jnp.int32, (16, 128), 1)
    cols0 = lax.broadcasted_iota(jnp.int32, (16, HV), 1) + v * VL

    def peer_copy(p, r):
        return pltpu.make_async_remote_copy(
            src_ref=msg.at[p],
            dst_ref=peers.at[p, r - 1],
            send_sem=st_s.at[p, r - 1],
            recv_sem=st_r.at[p, r - 1],
            device_id=(c, (v + r) % NV),
            device_id_type=pl.DeviceIdType.MESH,
        )

    def softmax(p):
        for h in (0, 1):
            pair_in(0, p, h)
        zr[p].arrive()

        @pl.loop(0, RP // 16)
        def _(r):
            at = pl.ds(pl.multiple_of(r * 16, 16), 16)
            t = tcol[pl.ds(pl.multiple_of(p * RP + r * 16, 16), 16), :]
            l0 = zr[p].total(0, 0, at)
            l1 = zr[p].total(1, 0, at)
            top = jnp.maximum(
                jnp.max(l0, axis=1, keepdims=True), jnp.max(l1, axis=1, keepdims=True)
            )
            hit = jnp.sum(jnp.where(cols0 == t, l0, 0.0), axis=1, keepdims=True) + jnp.sum(
                jnp.where(cols0 + HV == t, l1, 0.0), axis=1, keepdims=True
            )
            e0 = jnp.exp(l0 - top)
            e1 = jnp.exp(l1 - top)
            total = jnp.sum(e0, axis=1, keepdims=True) + jnp.sum(e1, axis=1, keepdims=True)
            logit[p, 0, at, :] = e0
            logit[p, 1, at, :] = e1
            stat[at, :] = jnp.where(lanes == 0, top, jnp.where(lanes == 1, total, hit))

        msg[p] = jnp.transpose(stat[...])[:8]

        @pl.loop(1, NV)
        def _(r):
            peer_copy(p, r).start()

    def gradient(p):
        @pl.loop(1, NV)
        def _(r):
            peer_copy(p, r).wait_recv()

        top, total, hit = msg[p, 0:1, :], msg[p, 1:2, :], msg[p, 2:3, :]
        tops = peers[p, :, 0, :]
        best = jnp.maximum(top, jnp.max(tops, axis=0, keepdims=True))
        everyone = total * jnp.exp(top - best) + jnp.sum(
            peers[p, :, 1, :] * jnp.exp(tops - best), axis=0, keepdims=True
        )
        hits = hit + jnp.sum(peers[p, :, 2, :], axis=0, keepdims=True)
        loss = jnp.log(everyone) + best - hits
        scale = jnp.exp(top - best) / everyone
        odd = lax.broadcasted_iota(jnp.int32, (128, 128), 0) % 2 == 1
        lcol[...] = jnp.transpose(jnp.where(odd, loss, scale))
        spot = lax.broadcasted_iota(jnp.int32, (RP, ROWS // 2), 1) * 2
        line = lax.broadcasted_iota(jnp.int32, (RP, ROWS // 2), 0) + p * RP
        for d in (0, 1):
            found = jnp.sum(
                jnp.where(line == spot + d, lcol[:RP, 1:2], 0.0), axis=0, keepdims=True
            )
            loss_out[d : d + 1, :] = found if p == 0 else loss_out[d : d + 1, :] + found

        @pl.loop(0, RP // 16)
        def _(r):
            at = pl.ds(pl.multiple_of(r * 16, 16), 16)
            here = pl.ds(pl.multiple_of(p * RP + r * 16, 16), 16)
            t = tcol[here, :]
            w = wcol[here, :]
            s = lcol[at, 0:1]
            for h in (0, 1):
                one = (cols0 + h * HV == t).astype(F32)
                dl[zh, core, here, h * HV : (h + 1) * HV] = (
                    w * (logit[p, h, at, :] * s - one)
                ).astype(BF16)

    class Gather:
        def __init__(self, p):
            self.p, self.base = p, sem2 + 9 * p
            self.all = pl.ds(p * RP, RP)
            self.first = pl.ds(p * RP, RP // 2)
            self.last = pl.ds(p * RP + RP // 2, RP // 2)

        def go(self, d, k, rows, i, dev):
            slot = dl.at[up(zh, d), k, rows]
            start(slot, slot, self.base + i, dev)

        def come(self, d, k, rows, i):
            slot = dl.at[up(zh, d), k, rows]
            rdma(slot, slot, self.base + i, partner).wait_recv()

        def begin(self):
            self.go(0, core, self.all, 0, dev_zh(1))
            self.go(0, core, self.all, 1, dev_zh(3))
            self.go(0, core, self.all, 2, partner)

        def near(self):
            self.come(3, core, self.all, 0)
            self.go(3, core, self.first, 3, dev_zh(1))
            self.come(1, core, self.all, 1)
            self.go(1, core, self.last, 5, dev_zh(3))
            self.go(3, core, self.all, 4, partner)
            self.go(1, core, self.all, 6, partner)

        def far(self):
            self.come(2, core, self.first, 3)
            self.go(2, core, self.first, 7, partner)
            self.come(2, core, self.last, 5)
            self.go(2, core, self.last, 8, partner)

        def backward(self, *ds):
            other = 1 - core
            for d in ds:
                if d == 2:
                    self.come(2, other, self.first, 7)
                    self.come(2, other, self.last, 8)
                else:
                    self.come(d, other, self.all, {0: 2, 3: 4, 1: 6}[d])
            lhs = [dl[up(zh, d), k, self.all] for d in ds for k in (0, 1)]
            lhs = jnp.concatenate(lhs, axis=0)
            for j in range(4):
                res = lax.dot_general(
                    lhs,
                    head[j * WIDTH : (j + 1) * WIDTH, :],
                    (((1,), (1,)), ((), ())),
                    preferred_element_type=F32,
                )
                for i, d in enumerate(ds):
                    at = up(up(zh, d), zh)
                    for k in (0, 1):
                        lo = (2 * i + k) * RP
                        g[at, 2 * k + j // 2, j % 2, self.all] = res[lo : lo + RP]

    class Collect:
        def __init__(self, p):
            self.p = p
            base = sem2 + 9 * NP + 32 * p
            self.base = base

            def here(at, lo=0):
                return pl.ds(p * RP + lo + at.start, at.size)

            self.here = here

            def ring(i, k, value, tiles, rows, code, dev):
                return Ring4Sum(
                    kit,
                    base + 12 * i,
                    value,
                    tiles,
                    rows,
                    rows,
                    (code.at[p, k, 0], code.at[p, k, 1]),
                    (sides.at[p, 1 + i, 0], sides.at[p, 1 + i, 1], cols.at[1 + k]),
                    dev(1),
                    dev(3),
                )

            self.one = (
                ring(0, 0, lambda d, h, t, at: g[2 * h + t, up(y, d), 0, here(at), :], 2, RP, code1, dev_y),
                ring(1, 1, lambda d, h, t, at: g[up(x, d), 2 * h + t, 1, here(at), :], 2, RP, code1, dev_x),
            )

        def straight(self, k, d):
            rows = pl.ds(self.p * RP, RP)
            if k == 0:
                src, dev = g.at[up(x, d), y, 0, rows], dev_x(d)
            else:
                src, dev = g.at[x, up(y, d), 1, rows], dev_y(d)
            return src, land2.at[self.p, k, d - 1], self.base + 24 + 3 * k + d - 1, dev

        def begin_two(self):
            for d in (2, 1, 3):
                for k in (0, 1):
                    start(*self.straight(k, d))

        def begin(self, stage):
            for i in (0, 1, 2, 3):
                for s in stage:
                    s.send(i)

        def relay(self, stage):
            for s in stage:
                s.relay()

        def end_one(self):
            for k, s in enumerate(self.one):
                s.arrive()

                at = pl.ds(0, RP)
                for h in (0, 1):
                    for t in (0, 1):
                        val = s.total(h, t, at)
                        if k == 0:
                            g[2 * h + t, y, 0, self.here(at), :] = val
                        else:
                            g[x, 2 * h + t, 1, self.here(at), :] = val

        def end_two(self):
            for k in (0, 1):
                for d in (1, 2, 3):
                    rdma(*self.straight(k, d)).wait_recv()
            for k in (0, 1):
                rows = pl.ds(self.p * RP, RP)
                total = g[x, y, k, rows]
                for d in range(3):
                    total = total + land2[self.p, k, d]
                g[x, y, k, rows] = total

            rows = pl.ds(self.p * RP, RP)
            start(g.at[x, y, 1 - zl, rows], zbuf.at[self.p], self.base + 30, dev_zl)

        def out(self):
            rows = pl.ds(self.p * RP, RP)
            rdma(g.at[x, y, 1 - zl, rows], zbuf.at[self.p], self.base + 30, dev_zl).wait_recv()
            obuf[self.p] = (g[x, y, zl, rows] + zbuf[self.p]).astype(BF16)
            src, dst = obuf.at[self.p], obuf_in.at[self.p]

            @pl.when(is_self)
            def _():
                pltpu.make_async_copy(src, dst, lsem.at[2 + self.p]).start()

            @pl.when(jnp.logical_not(is_self))
            def _():
                rdma(src, dst, self.base + 31, owner).start()

        def done(self):
            src, dst = obuf.at[self.p], obuf_in.at[self.p]

            @pl.when(is_self)
            def _():
                pltpu.make_async_copy(src, dst, lsem.at[2 + self.p]).wait()

            @pl.when(jnp.logical_not(is_self))
            def _():
                rdma(src, dst, self.base + 31, owner).wait()

            grad_out[self.p * RP : (self.p + 1) * RP, :] = obuf_in[self.p]

    ga, gb = Gather(0), Gather(1)
    ea, eb = Collect(0), Collect(1)
    softmax(0)
    zr[1].relay()
    gradient(0)
    ga.begin()
    softmax(1)
    ga.backward(0)
    ga.near()
    gradient(1)
    gb.begin()
    ga.backward(3, 1)
    ga.far()
    ga.backward(2)
    ea.begin(ea.one)
    gb.backward(0)
    ea.relay(ea.one)
    gb.near()
    ea.end_one()
    ea.begin_two()
    gb.backward(3, 1)
    gb.far()
    gb.backward(2)
    eb.begin(eb.one)
    ea.end_two()
    eb.relay(eb.one)
    ea.out()
    eb.end_one()
    eb.begin_two()
    eb.end_two()
    eb.out()
    ea.done()
    eb.done()

    for cp in kit.pending:
        cp.wait_send()

    for p in range(NP):

        @pl.loop(1, NV)
        def _(r):
            peer_copy(p, r).wait_send()


NSEM = 34 + 8 * NP + 12 * NP + 9 * NP + 32 * NP


def body(hidden, head, targets, loss_weight):
    tile = (ROWS, WIDTH)
    vmem = pl.BlockSpec(memory_space=pltpu.VMEM)
    loss, grad = pl.pallas_call(
        kernel,
        out_shape=(
            jax.ShapeDtypeStruct((2, ROWS // 2), F32),
            jax.ShapeDtypeStruct(tile, BF16),
        ),
        in_specs=[vmem, pl.BlockSpec(memory_space=pl.ANY), vmem, vmem],
        out_specs=(vmem, vmem),
        scratch_shapes=[
            pltpu.VMEM((RING, RING, 2, *tile), BF16),
            pltpu.VMEM((SLAB, VL), BF16),
            pltpu.VMEM((RING, 2, NP, 2, RP, HV), F32),
            pltpu.VMEM((RING, NP, 2, RP, HV), F32),
            pltpu.VMEM((NP, 2, 6, 1, RP, HV), I16),
            pltpu.VMEM((NP, 2, RP, HV), F32),
            pltpu.VMEM((ROWS, 128), F32),
            pltpu.VMEM((ROWS, 1), jnp.int32),
            pltpu.VMEM((ROWS, 1), F32),
            pltpu.VMEM((ROWS, 128), F32),
            pltpu.VMEM((NP, 8, ROWS), F32),
            pltpu.VMEM((NP, NV - 1, 8, ROWS), F32),
            pltpu.VMEM((RING, 2, ROWS, VL), BF16),
            pltpu.VMEM((RING, RING, 2, *tile), F32),
            pltpu.VMEM((NP, 2, 2, 6, 2, RP, WIDTH), I16),
            pltpu.VMEM((NP, 2, 3, RP, WIDTH), F32),
            pltpu.VMEM((NP, 3, 2, 6, 8, 128), F32),
            pltpu.VMEM((3, 6, 128, 128), F32),
            pltpu.VMEM((NP, RP, WIDTH), F32),
            pltpu.VMEM((NP, RP, WIDTH), BF16),
            pltpu.VMEM((NP, RP, WIDTH), BF16),
            pltpu.SemaphoreType.DMA((NSEM,)),
            pltpu.SemaphoreType.DMA((NSEM,)),
            pltpu.SemaphoreType.DMA((NP, NV - 1)),
            pltpu.SemaphoreType.DMA((NP, NV - 1)),
            pltpu.SemaphoreType.DMA((2 + NP,)),
        ],
        compiler_params=pltpu.CompilerParams(
            collective_id=0, has_side_effects=True, vmem_limit_bytes=60 * 1024 * 1024
        ),
        name="mtp_loss",
    )(hidden.reshape(tile), head, targets.T, loss_weight.T)
    rows, depths = targets.shape
    return loss.T, grad.reshape(rows, depths, WIDTH)


def solution(mesh):
    return jax.shard_map(
        body,
        mesh=mesh,
        in_specs=(P("ctx", None, "vocab"), P("ctx", "vocab"), P("ctx", None), P("ctx", None)),
        out_specs=(P("ctx", None), P("ctx", None, "vocab")),
        check_vma=False,
    )
```

```python
import jax
import jax.numpy as jnp
from jax import lax
from jax.experimental import pallas as pl
from jax.experimental.pallas import tpu as pltpu
from jax.sharding import PartitionSpec as P

F32 = jnp.float32
BF16 = jnp.bfloat16
RING = 4
NV = 32
ROWS = 128
WIDTH = 224
VL = 2048
HV = VL // 2
SLAB = 4 * WIDTH
NP = 2
PLAIN = (0,)
RP = ROWS // NP
I16 = jnp.int16
LEVELS = 32766.0
HOPS = ((2, 0, 0), (2, 1, 1), (3, 1, 0), (1, 0, 1), (3, 0, 0), (1, 1, 1))


class Ring4Sum:
    def __init__(self, k, base, value, tiles, rows, block, coded, sides, plus, minus):
        self.k, self.base, self.value = k, base, value
        self.tiles, self.rows, self.block = tiles, rows, block
        (self.out, self.land), (self.sout, self.sland, self.cols) = coded, sides
        self.plus, self.minus = plus, minus

    def copies(self, i):
        dev = self.plus if HOPS[i][2] else self.minus
        b = self.base + 2 * i
        return (
            self.k.rdma(self.out.at[i], self.land.at[i], b, dev),
            self.k.rdma(self.sout.at[i], self.sland.at[i], b + 1, dev),
        )

    def send(self, i, landed=()):
        d, h, _ = HOPS[i]
        stat = self.k.stat
        lanes = lax.broadcasted_iota(jnp.int32, (self.block, 128), 1)

        for r in range(self.rows // self.block):
            at = pl.ds(r * self.block, self.block)
            side = jnp.zeros((self.block, 128), F32)
            for t in range(self.tiles):
                val = self.value(d, h, t, at)
                for j in landed:
                    val = val + self.decoded(j, t, at)
                low = jnp.min(val, axis=1, keepdims=True)
                high = jnp.max(val, axis=1, keepdims=True)
                middle = 0.5 * low + 0.5 * high
                span = jnp.maximum(0.5 * high - 0.5 * low, 1e-30)
                steps = jnp.clip(jnp.round((val - middle) * (LEVELS / span)), -LEVELS, LEVELS)
                self.out[i, t, at, :] = steps.astype(jnp.int32).astype(I16)
                side = jnp.where(lanes == 2 * t, middle, side)
                side = jnp.where(lanes == 2 * t + 1, span * (1.0 / LEVELS), side)
            stat[at, :] = side

        self.sout[i] = jnp.transpose(stat[...])[:8]
        for cp in self.copies(i):
            cp.start()
            self.k.pending.append(cp)

    def receive(self, i):
        for cp in self.copies(i):
            cp.wait_recv()
        rows = jnp.concatenate([self.sland[i]] * 16, axis=0)
        self.cols[i] = jnp.transpose(rows)

    def decoded(self, i, t, at):
        steps = self.land[i, t, at, :].astype(jnp.int32).astype(F32)
        return steps * self.cols[i, at, 2 * t + 1 : 2 * t + 2] + self.cols[i, at, 2 * t : 2 * t + 1]

    def relay(self):
        self.receive(0)
        self.send(4, (0,))
        self.receive(1)
        self.send(5, (1,))

    def arrive(self):
        for i in (2, 3, 4, 5):
            self.receive(i)

    def total(self, h, t, at):
        i, j = ((3, 4), (2, 5))[h]
        return self.value(0, h, t, at) + self.decoded(i, t, at) + self.decoded(j, t, at)


class PlainSum(Ring4Sum):
    def __init__(self, k, base, part, land, plus, minus):
        self.k, self.base, self.part, self.land = k, base, part, land
        self.plus, self.minus = plus, minus

    def copies(self, i):
        d, h, to_plus = HOPS[i]
        dev = self.plus if to_plus else self.minus
        return (self.k.rdma(self.part(d, h), self.land.at[i], self.base + 2 * i, dev),)

    def send(self, i, landed=()):
        part = self.part(*HOPS[i][:2])
        for j in landed:
            part[...] = part[...] + self.land[j]
        for cp in self.copies(i):
            cp.start()
            self.k.pending.append(cp)

    def receive(self, i):
        for cp in self.copies(i):
            cp.wait_recv()

    def total(self, h, t, at):
        i, j = ((3, 4), (2, 5))[h]
        return self.part(0, h)[t, at, :] + self.land[i, t, at, :] + self.land[j, t, at, :]


class Tools:
    def __init__(self, ssem, rsem, stat):
        self.ssem, self.rsem, self.stat, self.pending = ssem, rsem, stat, []

    def rdma(self, src, dst, i, dev):
        return pltpu.make_async_remote_copy(
            src_ref=src,
            dst_ref=dst,
            send_sem=self.ssem.at[i],
            recv_sem=self.rsem.at[i],
            device_id=dev,
            device_id_type=pl.DeviceIdType.MESH,
        )

    def start(self, src, dst, i, dev):
        cp = self.rdma(src, dst, i, dev)
        cp.start()
        self.pending.append(cp)


def kernel(
    hid,
    head_hbm,
    tgt,
    wgt,
    loss_out,
    grad_out,
    buf,
    head,
    part,
    pair,
    zcode,
    logit,
    stat,
    tcol,
    wcol,
    lcol,
    msg,
    peers,
    dl,
    g,
    code1,
    land1,
    land2,
    sides,
    cols,
    zbuf,
    obuf,
    flat,
    ssem,
    rsem,
    st_s,
    st_r,
    lsem,
):
    c = lax.axis_index("ctx")
    v = lax.axis_index("vocab")
    zh, core = c // 2, c % 2
    x, y, zl = v // 8, (v // 2) % 4, v % 2
    kit = Tools(ssem, rsem, stat)
    rdma, start = kit.rdma, kit.start

    def up(i, d):
        return (i + d) % RING

    def dev_zh(d):
        return (up(zh, d) * 2 + core, v)

    def dev_x(d):
        return (c, up(x, d) * 8 + y * 2 + zl)

    def dev_y(d):
        return (c, x * 8 + up(y, d) * 2 + zl)

    partner = (zh * 2 + 1 - core, v)
    dev_zl = (c, x * 8 + y * 2 + 1 - zl)
    hx, hy = up(x, zh), core * 2 + y % 2
    holder = (v // 4, hx * 8 + hy * 2 + zl)
    owner = (up(x, 4 - zh) * 2 + y // 2, 4 * c + v % 4)
    is_self = jnp.logical_and(holder[0] == c, holder[1] == v)

    head_copy = pltpu.make_async_copy(head_hbm, head, lsem.at[0])
    head_copy.start()

    barrier = pltpu.get_barrier_semaphore()

    def greet(dev):
        pl.semaphore_signal(barrier, inc=1, device_id=dev, device_id_type=pl.DeviceIdType.MESH)

    @pl.when(jnp.logical_not(is_self))
    def _():
        greet(holder)
        greet(owner)

    for dev in (
        partner,
        dev_zh(1),
        dev_zh(3),
        dev_x(1),
        dev_x(3),
        dev_y(1),
        dev_y(3),
        dev_zl,
    ):
        greet(dev)

    flat[...] = hid[...].reshape(ROWS, WIDTH)

    @pl.when(jnp.logical_not(is_self))
    def _():
        pl.semaphore_wait(barrier, 10)

    @pl.when(is_self)
    def _():
        pl.semaphore_wait(barrier, 8)

    @pl.when(is_self)
    def _():
        cp = pltpu.make_async_copy(flat, buf.at[x, y, zl], lsem.at[1])
        cp.start()
        cp.wait()

    @pl.when(jnp.logical_not(is_self))
    def _():
        cp = rdma(flat, buf.at[hx, hy, zl], 0, holder)
        cp.start()
        cp.wait_send()
        rdma(flat, buf.at[x, y, zl], 0, holder).wait_recv()

    start(buf.at[x, y, zl], buf.at[x, y, zl], 1, dev_zl)

    row = lax.broadcasted_iota(jnp.int32, (ROWS, ROWS // 2), 0)
    tok = lax.broadcasted_iota(jnp.int32, (ROWS, ROWS // 2), 1)

    def as_column(pairs):
        both = jnp.where(row % 2 == 1, pairs[1:2, :], pairs[0:1, :])
        return jnp.sum(jnp.where(row // 2 == tok, both, 0.0), axis=1, keepdims=True)

    tcol[...] = as_column(tgt[...].astype(F32)).astype(jnp.int32)
    wcol[...] = as_column(wgt[...])

    lines = (
        (lambda a, b: buf.at[a, b, 0], x, y, dev_x, dev_y),
        (lambda a, b: buf.at[b, a, 1], y, x, dev_y, dev_x),
    )
    steps = (0, 3, 1, 2)

    def second(k, n):
        at, a, b, dev_a, dev_b = lines[k]
        base = 2 + 16 * k
        for d, o in ((1, 4), (3, 8)):
            tile = at(up(a, steps[n]), b)
            start(tile, tile, base + o + n, dev_b(d))

    def second_in(k, n, d):
        at, a, b, dev_a, dev_b = lines[k]
        base = 2 + 16 * k
        tile = at(up(a, steps[n]), up(b, 4 - d))
        rdma(tile, tile, base + (4 if d == 1 else 8) + n, dev_b(d)).wait_recv()
        return tile

    def first(k):
        at, a, b, dev_a, dev_b = lines[k]
        base = 2 + 16 * k
        tile = at(a, b)
        return [
            rdma(tile, tile, base + i, dev)
            for i, dev in ((0, dev_a(1)), (1, dev_a(3)), (4, dev_b(1)), (8, dev_b(3)))
        ]

    def start_first(k):
        for cp in first(k):
            cp.start()

    for k in (0, 1):
        kit.pending.extend(first(k))
        pl.when(zl == k)(lambda: start_first(k))
    rdma(buf.at[x, y, zl], buf.at[x, y, 1 - zl], 1, dev_zl).wait_recv()
    for k in (1, 0):
        pl.when(zl != k)(lambda: start_first(k))
    for k, (at, a, b, dev_a, dev_b) in enumerate(lines):
        base = 2 + 16 * k
        for d, i, rows in ((1, 0, pl.ds(0, 64)), (3, 1, pl.ds(64, 64))):
            tile = at(up(a, 4 - d), b)
            rdma(tile, tile, base + i, dev_a(d)).wait_recv()
            half = tile.at[rows]
            start(half, half, base + 2 + i, dev_a(d))
            second(k, 1 + i)
    for k, (at, a, b, dev_a, dev_b) in enumerate(lines):
        base = 2 + 16 * k
        for d, i, rows in ((1, 0, pl.ds(0, 64)), (3, 1, pl.ds(64, 64))):
            half = at(up(a, 2), b).at[rows]
            rdma(half, half, base + 2 + i, dev_a(d)).wait_recv()
        second(k, 3)
    for n, d in ((0, 1), (1, 1), (2, 3), (3, 3)):
        for k, (at, a, b, dev_a, dev_b) in enumerate(lines):
            tile = second_in(k, n, d)
            start(tile, tile, 2 + 16 * k + 12 + n, dev_b(d))
    for k, (at, a, b, dev_a, dev_b) in enumerate(lines):
        for n, d in ((2, 1), (3, 1), (0, 3), (1, 3)):
            second_in(k, n, d)
        for n in range(4):
            tile = at(up(a, steps[n]), up(b, 2))
            rdma(tile, tile, 2 + 16 * k + 12 + n, dev_b(1)).wait_recv()
    sem = 34

    head_copy.wait()

    def forward(d, h):
        q = up(zh, d)
        at = up(q, zh)

        @pl.loop(0, HV // 256)
        def _(n):
            cs = pl.ds(pl.multiple_of(h * HV + n * 256, 256), 256)
            out_cs = pl.ds(pl.multiple_of(n * 256, 256), 256)
            acc = None
            for j in range(4):
                lhs = jnp.concatenate([buf[at, j // 2, j % 2], buf[at, 2 + j // 2, j % 2]], axis=0)
                term = jnp.dot(
                    lhs, head[j * WIDTH : (j + 1) * WIDTH, cs], preferred_element_type=F32
                )
                acc = term if acc is None else acc + term
            for k in range(2):
                for p in range(NP):
                    lo = k * ROWS + p * RP
                    part[q, k, p, h, :, out_cs] = acc[lo : lo + RP]

        for p in range(NP):
            start(part.at[q, 1 - core, p, h], pair.at[q, p, h], pair_sem(d, p, h), partner)

    def pair_sem(d, p, h):
        return sem + (d * NP + p) * 2 + h

    def pair_in(d, p, h):
        q = up(zh, d)
        rdma(part.at[q, 1 - core, p, h], pair.at[q, p, h], pair_sem(d, p, h), partner).wait_recv()

    zr = [
        Ring4Sum(
            kit,
            sem + 8 * NP + 12 * p,
            lambda d, h, t, at, p=p: part[up(zh, d), core, p, h, at, :]
            + pair[up(zh, d), p, h, at, :],
            1,
            RP,
            16,
            (zcode.at[p, 0], zcode.at[p, 1]),
            (sides.at[p, 0, 0], sides.at[p, 0, 1], cols.at[0]),
            dev_zh(1),
            dev_zh(3),
        )
        for p in range(NP)
    ]
    def logits_begin(p):
        for h in (0, 1):
            pair_in(2, p, h)
            zr[p].send(h)

    forward(2, 0)
    forward(2, 1)
    logits_begin(0)
    forward(3, 1)
    pair_in(3, 0, 1)
    zr[0].send(2)
    forward(1, 0)
    pair_in(1, 0, 0)
    zr[0].send(3)
    forward(3, 0)
    forward(1, 1)
    pair_in(3, 0, 0)
    pair_in(1, 0, 1)
    zr[0].relay()
    logits_begin(1)
    pair_in(3, 1, 1)
    zr[1].send(2)
    pair_in(1, 1, 0)
    zr[1].send(3)
    forward(0, 0)
    forward(0, 1)
    pair_in(3, 1, 0)
    pair_in(1, 1, 1)
    sem2 = sem + 8 * NP + 12 * NP

    lanes = lax.broadcasted_iota(jnp.int32, (16, 128), 1)
    cols0 = lax.broadcasted_iota(jnp.int32, (16, HV), 1) + v * VL

    def peer_copy(p, r):
        return pltpu.make_async_remote_copy(
            src_ref=msg.at[p],
            dst_ref=peers.at[p, r - 1],
            send_sem=st_s.at[p, r - 1],
            recv_sem=st_r.at[p, r - 1],
            device_id=(c, (v + r) % NV),
            device_id_type=pl.DeviceIdType.MESH,
        )

    def softmax(p):
        for h in (0, 1):
            pair_in(0, p, h)
        zr[p].arrive()

        @pl.loop(0, RP // 16)
        def _(r):
            at = pl.ds(pl.multiple_of(r * 16, 16), 16)
            t = tcol[pl.ds(pl.multiple_of(p * RP + r * 16, 16), 16), :]
            l0 = zr[p].total(0, 0, at)
            l1 = zr[p].total(1, 0, at)
            top = jnp.maximum(
                jnp.max(l0, axis=1, keepdims=True), jnp.max(l1, axis=1, keepdims=True)
            )
            hit = jnp.sum(jnp.where(cols0 == t, l0, 0.0), axis=1, keepdims=True) + jnp.sum(
                jnp.where(cols0 + HV == t, l1, 0.0), axis=1, keepdims=True
            )
            e0 = jnp.exp(l0 - top)
            e1 = jnp.exp(l1 - top)
            total = jnp.sum(e0, axis=1, keepdims=True) + jnp.sum(e1, axis=1, keepdims=True)
            logit[p, 0, at, :] = e0
            logit[p, 1, at, :] = e1
            stat[at, :] = jnp.where(lanes == 0, top, jnp.where(lanes == 1, total, hit))

        msg[p] = jnp.transpose(stat[...])[:8]

        @pl.loop(1, NV)
        def _(r):
            peer_copy(p, r).start()

    def gradient(p):
        @pl.loop(1, NV)
        def _(r):
            peer_copy(p, r).wait_recv()

        top, total, hit = msg[p, 0:1, :], msg[p, 1:2, :], msg[p, 2:3, :]
        tops = peers[p, :, 0, :]
        best = jnp.maximum(top, jnp.max(tops, axis=0, keepdims=True))
        everyone = total * jnp.exp(top - best) + jnp.sum(
            peers[p, :, 1, :] * jnp.exp(tops - best), axis=0, keepdims=True
        )
        hits = hit + jnp.sum(peers[p, :, 2, :], axis=0, keepdims=True)
        loss = jnp.log(everyone) + best - hits
        scale = jnp.exp(top - best) / everyone
        odd = lax.broadcasted_iota(jnp.int32, (128, 128), 0) % 2 == 1
        lcol[...] = jnp.transpose(jnp.where(odd, loss, scale))
        spot = lax.broadcasted_iota(jnp.int32, (RP, ROWS // 2), 1) * 2
        line = lax.broadcasted_iota(jnp.int32, (RP, ROWS // 2), 0) + p * RP
        for d in (0, 1):
            found = jnp.sum(
                jnp.where(line == spot + d, lcol[:RP, 1:2], 0.0), axis=0, keepdims=True
            )
            loss_out[d : d + 1, :] = found if p == 0 else loss_out[d : d + 1, :] + found

        @pl.loop(0, RP // 16)
        def _(r):
            at = pl.ds(pl.multiple_of(r * 16, 16), 16)
            here = pl.ds(pl.multiple_of(p * RP + r * 16, 16), 16)
            t = tcol[here, :]
            w = wcol[here, :]
            s = lcol[at, 0:1]
            for h in (0, 1):
                one = (cols0 + h * HV == t).astype(F32)
                dl[zh, core, here, h * HV : (h + 1) * HV] = (
                    w * (logit[p, h, at, :] * s - one)
                ).astype(BF16)

    class Gather:
        def __init__(self, p):
            self.p, self.base = p, sem2 + 9 * p
            self.all = pl.ds(p * RP, RP)
            self.first = pl.ds(p * RP, RP // 2)
            self.last = pl.ds(p * RP + RP // 2, RP // 2)

        def go(self, d, k, rows, i, dev):
            slot = dl.at[up(zh, d), k, rows]
            start(slot, slot, self.base + i, dev)

        def come(self, d, k, rows, i):
            slot = dl.at[up(zh, d), k, rows]
            rdma(slot, slot, self.base + i, partner).wait_recv()

        def begin(self):
            self.go(0, core, self.all, 0, dev_zh(1))
            self.go(0, core, self.all, 1, dev_zh(3))
            self.go(0, core, self.all, 2, partner)

        def near(self):
            self.come(3, core, self.all, 0)
            self.go(3, core, self.first, 3, dev_zh(1))
            self.come(1, core, self.all, 1)
            self.go(1, core, self.last, 5, dev_zh(3))
            self.go(3, core, self.all, 4, partner)
            self.go(1, core, self.all, 6, partner)

        def far(self):
            self.come(2, core, self.first, 3)
            self.go(2, core, self.first, 7, partner)
            self.come(2, core, self.last, 5)
            self.go(2, core, self.last, 8, partner)

        def backward(self, *ds):
            other = 1 - core
            for d in ds:
                if d == 2:
                    self.come(2, other, self.first, 7)
                    self.come(2, other, self.last, 8)
                else:
                    self.come(d, other, self.all, {0: 2, 3: 4, 1: 6}[d])
            lhs = [dl[up(zh, d), k, self.all] for d in ds for k in (0, 1)]
            lhs = jnp.concatenate(lhs, axis=0)
            for j in range(4):
                res = lax.dot_general(
                    lhs,
                    head[j * WIDTH : (j + 1) * WIDTH, :],
                    (((1,), (1,)), ((), ())),
                    preferred_element_type=F32,
                )
                for i, d in enumerate(ds):
                    at = up(up(zh, d), zh)
                    for k in (0, 1):
                        lo = (2 * i + k) * RP
                        g[at, 2 * k + j // 2, j % 2, self.all] = res[lo : lo + RP]

    class Collect:
        def __init__(self, p):
            self.p = p
            base = sem2 + 9 * NP + 32 * p
            self.base = base

            def here(at, lo=0):
                return pl.ds(p * RP + lo + at.start, at.size)

            self.here = here

            def ring(i, k, value, tiles, rows, code, dev):
                return Ring4Sum(
                    kit,
                    base + 12 * i,
                    value,
                    tiles,
                    rows,
                    rows,
                    (code.at[p, k, 0], code.at[p, k, 1]),
                    (sides.at[p, 1 + i, 0], sides.at[p, 1 + i, 1], cols.at[1 + k]),
                    dev(1),
                    dev(3),
                )

            rows = pl.ds(p * RP, RP)
            if p in PLAIN:
                self.one = (
                    PlainSum(
                        kit,
                        base,
                        lambda d, h: g.at[pl.ds(up(2 * h, 2 * zh), 2), up(y, d), 0, rows],
                        land1.at[p, 0],
                        dev_y(1),
                        dev_y(3),
                    ),
                    PlainSum(
                        kit,
                        base + 12,
                        lambda d, h: g.at[up(x, d), pl.ds(2 * h, 2), 1, rows],
                        land1.at[p, 1],
                        dev_x(1),
                        dev_x(3),
                    ),
                )
                return
            self.one = (
                ring(0, 0, lambda d, h, t, at: g[up(2 * h + t, 2 * zh), up(y, d), 0, here(at), :], 2, RP, code1, dev_y),
                ring(1, 1, lambda d, h, t, at: g[up(x, d), 2 * h + t, 1, here(at), :], 2, RP, code1, dev_x),
            )

        def straight(self, k, d):
            rows = pl.ds(self.p * RP, RP)
            if k == 0:
                src, dev = g.at[up(x, d), y, 0, rows], dev_x(d)
            else:
                src, dev = g.at[x, up(y, d), 1, rows], dev_y(d)
            return src, land2.at[self.p, k, d - 1], self.base + 24 + 3 * k + d - 1, dev

        def begin_two(self):
            for d in (2, 1, 3):
                for k in (0, 1):
                    start(*self.straight(k, d))

        def begin(self, stage):
            for i in (0, 1, 2, 3):
                for s in stage:
                    s.send(i)

        def begin_early(self):
            for i in (0, 3):
                self.one[0].send(i)

        def begin_late(self):
            self.one[0].send(1)
            self.one[1].send(0)
            self.one[0].send(2)
            for i in (1, 2, 3):
                self.one[1].send(i)

        def relay(self, stage):
            for s in stage:
                s.relay()

        def end_one(self):
            for k, s in enumerate(self.one):
                s.arrive()

                at = pl.ds(0, RP)
                for h in (0, 1):
                    for t in (0, 1):
                        val = s.total(h, t, at)
                        if k == 0:
                            g[up(2 * h + t, 2 * zh), y, 0, self.here(at), :] = val
                        else:
                            g[x, 2 * h + t, 1, self.here(at), :] = val

        def end_two(self):
            for k in (0, 1):
                for d in (1, 2, 3):
                    rdma(*self.straight(k, d)).wait_recv()
            for k in (0, 1):
                rows = pl.ds(self.p * RP, RP)
                total = g[x, y, k, rows]
                for d in range(3):
                    total = total + land2[self.p, k, d]
                g[x, y, k, rows] = total

            rows = pl.ds(self.p * RP, RP)
            start(g.at[x, y, 1 - zl, rows], zbuf.at[self.p], self.base + 30, dev_zl)

        def out(self):
            rows = pl.ds(self.p * RP, RP)
            rdma(g.at[x, y, 1 - zl, rows], zbuf.at[self.p], self.base + 30, dev_zl).wait_recv()
            obuf[self.p] = (g[x, y, zl, rows] + zbuf[self.p]).astype(BF16)
            src, dst = obuf.at[self.p], grad_out.at[rows]

            @pl.when(is_self)
            def _():
                pltpu.make_async_copy(src, dst, lsem.at[2 + self.p]).start()

            @pl.when(jnp.logical_not(is_self))
            def _():
                rdma(src, dst, self.base + 31, owner).start()

        def done(self):
            rows = pl.ds(self.p * RP, RP)
            src, dst = obuf.at[self.p], grad_out.at[rows]

            @pl.when(is_self)
            def _():
                pltpu.make_async_copy(src, dst, lsem.at[2 + self.p]).wait()

            @pl.when(jnp.logical_not(is_self))
            def _():
                rdma(src, dst, self.base + 31, owner).wait()

    ga, gb = Gather(0), Gather(1)
    ea, eb = Collect(0), Collect(1)
    softmax(0)
    zr[1].relay()
    gradient(0)
    ga.begin()
    softmax(1)
    ga.backward(0)
    ga.near()
    gradient(1)
    gb.begin()
    ga.backward(3, 1)
    ga.far()
    ga.backward(2)
    ea.begin(ea.one)
    gb.backward(0)
    ea.relay(ea.one)
    gb.near()
    ea.end_one()
    ea.begin_two()
    gb.backward(3, 1)
    gb.far()
    eb.begin_early()
    gb.backward(2)
    eb.begin_late()
    ea.end_two()
    eb.relay(eb.one)
    ea.out()
    eb.end_one()
    eb.begin_two()
    eb.end_two()
    eb.out()
    ea.done()
    eb.done()

    for cp in kit.pending:
        cp.wait_send()

    for p in range(NP):

        @pl.loop(1, NV)
        def _(r):
            peer_copy(p, r).wait_send()


NSEM = 34 + 8 * NP + 12 * NP + 9 * NP + 32 * NP


def body(hidden, head, targets, loss_weight):
    tile = (ROWS, WIDTH)
    vmem = pl.BlockSpec(memory_space=pltpu.VMEM)
    loss, grad = pl.pallas_call(
        kernel,
        out_shape=(
            jax.ShapeDtypeStruct((2, ROWS // 2), F32),
            jax.ShapeDtypeStruct(tile, BF16),
        ),
        in_specs=[vmem, pl.BlockSpec(memory_space=pl.ANY), vmem, vmem],
        out_specs=(vmem, pl.BlockSpec(memory_space=pl.ANY)),
        scratch_shapes=[
            pltpu.VMEM((RING, RING, 2, *tile), BF16),
            pltpu.VMEM((SLAB, VL), BF16),
            pltpu.VMEM((RING, 2, NP, 2, RP, HV), F32),
            pltpu.VMEM((RING, NP, 2, RP, HV), F32),
            pltpu.VMEM((NP, 2, 6, 1, RP, HV), I16),
            pltpu.VMEM((NP, 2, RP, HV), F32),
            pltpu.VMEM((ROWS, 128), F32),
            pltpu.VMEM((ROWS, 1), jnp.int32),
            pltpu.VMEM((ROWS, 1), F32),
            pltpu.VMEM((ROWS, 128), F32),
            pltpu.VMEM((NP, 8, ROWS), F32),
            pltpu.VMEM((NP, NV - 1, 8, ROWS), F32),
            pltpu.VMEM((RING, 2, ROWS, VL), BF16),
            pltpu.VMEM((RING, RING, 2, *tile), F32),
            pltpu.VMEM((NP, 2, 2, 6, 2, RP, WIDTH), I16),
            pltpu.VMEM((NP, 2, 6, 2, RP, WIDTH), F32),
            pltpu.VMEM((NP, 2, 3, RP, WIDTH), F32),
            pltpu.VMEM((NP, 3, 2, 6, 8, 128), F32),
            pltpu.VMEM((3, 6, 128, 128), F32),
            pltpu.VMEM((NP, RP, WIDTH), F32),
            pltpu.VMEM((NP, RP, WIDTH), BF16),
            pltpu.VMEM(tile, BF16),
            pltpu.SemaphoreType.DMA((NSEM,)),
            pltpu.SemaphoreType.DMA((NSEM,)),
            pltpu.SemaphoreType.DMA((NP, NV - 1)),
            pltpu.SemaphoreType.DMA((NP, NV - 1)),
            pltpu.SemaphoreType.DMA((2 + NP,)),
        ],
        compiler_params=pltpu.CompilerParams(
            collective_id=0, has_side_effects=True, vmem_limit_bytes=60 * 1024 * 1024
        ),
        name="mtp_loss",
    )(hidden, head, targets.T, loss_weight.T)
    rows, depths = targets.shape
    return loss.T, grad.reshape(rows, depths, WIDTH)


def solution(mesh):
    return jax.shard_map(
        body,
        mesh=mesh,
        in_specs=(P("ctx", None, "vocab"), P("ctx", "vocab"), P("ctx", None), P("ctx", None)),
        out_specs=(P("ctx", None), P("ctx", None, "vocab")),
        check_vma=False,
    )
```

```python
import jax
import jax.numpy as jnp
from jax import lax
from jax.experimental import pallas as pl
from jax.experimental.pallas import tpu as pltpu
from jax.sharding import PartitionSpec as P

F32 = jnp.float32
BF16 = jnp.bfloat16
RING = 4
NV = 32
ROWS = 128
WIDTH = 224
VL = 2048
HV = VL // 2
SLAB = 4 * WIDTH
NP = 2
PLAIN = (0,)
RP = ROWS // NP
I16 = jnp.int16
LEVELS = 32766.0
HOPS = ((2, 0, 0), (2, 1, 1), (3, 1, 0), (1, 0, 1), (3, 0, 0), (1, 1, 1))


class Ring4Sum:
    def __init__(self, k, base, value, tiles, rows, block, coded, sides, plus, minus):
        self.k, self.base, self.value = k, base, value
        self.tiles, self.rows, self.block = tiles, rows, block
        (self.out, self.land), (self.sout, self.sland, self.cols) = coded, sides
        self.plus, self.minus = plus, minus

    def copies(self, i):
        dev = self.plus if HOPS[i][2] else self.minus
        b = self.base + 2 * i
        return (
            self.k.rdma(self.out.at[i], self.land.at[i], b, dev),
            self.k.rdma(self.sout.at[i], self.sland.at[i], b + 1, dev),
        )

    def send(self, i, landed=()):
        d, h, _ = HOPS[i]
        stat = self.k.stat
        lanes = lax.broadcasted_iota(jnp.int32, (self.block, 128), 1)

        for r in range(self.rows // self.block):
            at = pl.ds(r * self.block, self.block)
            side = jnp.zeros((self.block, 128), F32)
            for t in range(self.tiles):
                val = self.value(d, h, t, at)
                for j in landed:
                    val = val + self.decoded(j, t, at)
                low = jnp.min(val, axis=1, keepdims=True)
                high = jnp.max(val, axis=1, keepdims=True)
                middle = 0.5 * low + 0.5 * high
                span = jnp.maximum(0.5 * high - 0.5 * low, 1e-30)
                steps = jnp.clip(jnp.round((val - middle) * (LEVELS / span)), -LEVELS, LEVELS)
                self.out[i, t, at, :] = steps.astype(jnp.int32).astype(I16)
                side = jnp.where(lanes == 2 * t, middle, side)
                side = jnp.where(lanes == 2 * t + 1, span * (1.0 / LEVELS), side)
            stat[at, :] = side

        self.sout[i] = jnp.transpose(stat[...])[:8]
        for cp in self.copies(i):
            cp.start()
            self.k.pending.append(cp)

    def receive(self, i):
        for cp in self.copies(i):
            cp.wait_recv()
        rows = jnp.concatenate([self.sland[i]] * 16, axis=0)
        self.cols[i] = jnp.transpose(rows)

    def decoded(self, i, t, at):
        steps = self.land[i, t, at, :].astype(jnp.int32).astype(F32)
        return steps * self.cols[i, at, 2 * t + 1 : 2 * t + 2] + self.cols[i, at, 2 * t : 2 * t + 1]

    def relay(self):
        self.receive(0)
        self.send(4, (0,))
        self.receive(1)
        self.send(5, (1,))

    def arrive(self):
        for i in (2, 3, 4, 5):
            self.receive(i)

    def total(self, h, t, at):
        i, j = ((3, 4), (2, 5))[h]
        return self.value(0, h, t, at) + self.decoded(i, t, at) + self.decoded(j, t, at)


class PlainSum(Ring4Sum):
    def __init__(self, k, base, part, land, plus, minus):
        self.k, self.base, self.part, self.land = k, base, part, land
        self.plus, self.minus = plus, minus

    def copies(self, i):
        d, h, to_plus = HOPS[i]
        dev = self.plus if to_plus else self.minus
        return (self.k.rdma(self.part(d, h), self.land.at[i], self.base + 2 * i, dev),)

    def send(self, i, landed=()):
        part = self.part(*HOPS[i][:2])
        for j in landed:
            part[...] = part[...] + self.land[j]
        for cp in self.copies(i):
            cp.start()
            self.k.pending.append(cp)

    def receive(self, i):
        for cp in self.copies(i):
            cp.wait_recv()

    def total(self, h, t, at):
        i, j = ((3, 4), (2, 5))[h]
        return self.part(0, h)[t, at, :] + self.land[i, t, at, :] + self.land[j, t, at, :]


class Tools:
    def __init__(self, ssem, rsem, stat):
        self.ssem, self.rsem, self.stat, self.pending = ssem, rsem, stat, []

    def rdma(self, src, dst, i, dev):
        return pltpu.make_async_remote_copy(
            src_ref=src,
            dst_ref=dst,
            send_sem=self.ssem.at[i],
            recv_sem=self.rsem.at[i],
            device_id=dev,
            device_id_type=pl.DeviceIdType.MESH,
        )

    def start(self, src, dst, i, dev):
        cp = self.rdma(src, dst, i, dev)
        cp.start()
        self.pending.append(cp)


def kernel(
    hid,
    head_hbm,
    tgt,
    wgt,
    loss_out,
    grad_out,
    buf,
    head,
    part,
    pair,
    zcode,
    logit,
    stat,
    tcol,
    wcol,
    lcol,
    msg,
    peers,
    dl,
    g,
    code1,
    land1,
    land2,
    sides,
    cols,
    zbuf,
    obuf,
    flat,
    ssem,
    rsem,
    st_s,
    st_r,
    lsem,
):
    c = lax.axis_index("ctx")
    v = lax.axis_index("vocab")
    zh, core = c // 2, c % 2
    x, y, zl = v // 8, (v // 2) % 4, v % 2
    kit = Tools(ssem, rsem, stat)
    rdma, start = kit.rdma, kit.start

    def up(i, d):
        return (i + d) % RING

    def dev_zh(d):
        return (up(zh, d) * 2 + core, v)

    def dev_x(d):
        return (c, up(x, d) * 8 + y * 2 + zl)

    def dev_y(d):
        return (c, x * 8 + up(y, d) * 2 + zl)

    partner = (zh * 2 + 1 - core, v)
    dev_zl = (c, x * 8 + y * 2 + 1 - zl)
    hx, hy = up(x, zh), core * 2 + y % 2
    holder = (v // 4, hx * 8 + hy * 2 + zl)
    owner = (up(x, 4 - zh) * 2 + y // 2, 4 * c + v % 4)
    is_self = jnp.logical_and(holder[0] == c, holder[1] == v)

    head_copy = pltpu.make_async_copy(head_hbm, head, lsem.at[0])
    head_copy.start()

    barrier = pltpu.get_barrier_semaphore()

    def greet(dev):
        pl.semaphore_signal(barrier, inc=1, device_id=dev, device_id_type=pl.DeviceIdType.MESH)

    @pl.when(jnp.logical_not(is_self))
    def _():
        greet(holder)
        greet(owner)

    for dev in (
        partner,
        dev_zh(1),
        dev_zh(3),
        dev_x(1),
        dev_x(3),
        dev_y(1),
        dev_y(3),
        dev_zl,
    ):
        greet(dev)

    flat[...] = hid[...].reshape(ROWS, WIDTH)

    @pl.when(jnp.logical_not(is_self))
    def _():
        pl.semaphore_wait(barrier, 10)

    @pl.when(is_self)
    def _():
        pl.semaphore_wait(barrier, 8)

    @pl.when(is_self)
    def _():
        cp = pltpu.make_async_copy(flat, buf.at[x, y, zl], lsem.at[1])
        cp.start()
        cp.wait()

    @pl.when(jnp.logical_not(is_self))
    def _():
        cp = rdma(flat, buf.at[hx, hy, zl], 0, holder)
        cp.start()
        cp.wait_send()
        rdma(flat, buf.at[x, y, zl], 0, holder).wait_recv()

    start(buf.at[x, y, zl], buf.at[x, y, zl], 1, dev_zl)

    row = lax.broadcasted_iota(jnp.int32, (ROWS, ROWS // 2), 0)
    tok = lax.broadcasted_iota(jnp.int32, (ROWS, ROWS // 2), 1)

    def as_column(pairs):
        both = jnp.where(row % 2 == 1, pairs[1:2, :], pairs[0:1, :])
        return jnp.sum(jnp.where(row // 2 == tok, both, 0.0), axis=1, keepdims=True)

    tcol[...] = as_column(tgt[...].astype(F32)).astype(jnp.int32)
    wcol[...] = as_column(wgt[...])

    lines = (
        (lambda a, b: buf.at[a, b, 0], x, y, dev_x, dev_y),
        (lambda a, b: buf.at[b, a, 1], y, x, dev_y, dev_x),
    )
    steps = (0, 3, 1, 2)

    def second(k, n):
        at, a, b, dev_a, dev_b = lines[k]
        base = 2 + 16 * k
        for d, o in ((1, 4), (3, 8)):
            tile = at(up(a, steps[n]), b)
            start(tile, tile, base + o + n, dev_b(d))

    def second_in(k, n, d):
        at, a, b, dev_a, dev_b = lines[k]
        base = 2 + 16 * k
        tile = at(up(a, steps[n]), up(b, 4 - d))
        rdma(tile, tile, base + (4 if d == 1 else 8) + n, dev_b(d)).wait_recv()
        return tile

    def first(k):
        at, a, b, dev_a, dev_b = lines[k]
        base = 2 + 16 * k
        tile = at(a, b)
        return [
            rdma(tile, tile, base + i, dev)
            for i, dev in ((0, dev_a(1)), (1, dev_a(3)), (4, dev_b(1)), (8, dev_b(3)))
        ]

    def start_first(k):
        for cp in first(k):
            cp.start()

    for k in (0, 1):
        kit.pending.extend(first(k))
        pl.when(zl == k)(lambda: start_first(k))
    rdma(buf.at[x, y, zl], buf.at[x, y, 1 - zl], 1, dev_zl).wait_recv()
    for k in (1, 0):
        pl.when(zl != k)(lambda: start_first(k))
    for k, (at, a, b, dev_a, dev_b) in enumerate(lines):
        base = 2 + 16 * k
        for d, i, rows in ((1, 0, pl.ds(0, 64)), (3, 1, pl.ds(64, 64))):
            tile = at(up(a, 4 - d), b)
            rdma(tile, tile, base + i, dev_a(d)).wait_recv()
            half = tile.at[rows]
            start(half, half, base + 2 + i, dev_a(d))
            second(k, 1 + i)
    for k, (at, a, b, dev_a, dev_b) in enumerate(lines):
        base = 2 + 16 * k
        for d, i, rows in ((1, 0, pl.ds(0, 64)), (3, 1, pl.ds(64, 64))):
            half = at(up(a, 2), b).at[rows]
            rdma(half, half, base + 2 + i, dev_a(d)).wait_recv()
        second(k, 3)
    for n, d in ((0, 1), (1, 1), (2, 3), (3, 3)):
        for k, (at, a, b, dev_a, dev_b) in enumerate(lines):
            tile = second_in(k, n, d)
            start(tile, tile, 2 + 16 * k + 12 + n, dev_b(d))
    for k, (at, a, b, dev_a, dev_b) in enumerate(lines):
        for n, d in ((2, 1), (3, 1), (0, 3), (1, 3)):
            second_in(k, n, d)
        for n in range(4):
            tile = at(up(a, steps[n]), up(b, 2))
            rdma(tile, tile, 2 + 16 * k + 12 + n, dev_b(1)).wait_recv()
    sem = 34

    head_copy.wait()

    def forward(d, h):
        q = up(zh, d)
        at = up(q, zh)

        @pl.loop(0, HV // 256)
        def _(n):
            cs = pl.ds(pl.multiple_of(h * HV + n * 256, 256), 256)
            out_cs = pl.ds(pl.multiple_of(n * 256, 256), 256)
            acc = None
            for j in range(4):
                lhs = jnp.concatenate([buf[at, j // 2, j % 2], buf[at, 2 + j // 2, j % 2]], axis=0)
                term = jnp.dot(
                    lhs, head[j * WIDTH : (j + 1) * WIDTH, cs], preferred_element_type=F32
                )
                acc = term if acc is None else acc + term
            for k in range(2):
                for p in range(NP):
                    lo = k * ROWS + p * RP
                    part[q, k, p, h, :, out_cs] = acc[lo : lo + RP]

        for p in range(NP):
            start(part.at[q, 1 - core, p, h], pair.at[q, p, h], pair_sem(d, p, h), partner)

    def pair_sem(d, p, h):
        return sem + (d * NP + p) * 2 + h

    def pair_in(d, p, h):
        q = up(zh, d)
        rdma(part.at[q, 1 - core, p, h], pair.at[q, p, h], pair_sem(d, p, h), partner).wait_recv()

    zr = [
        Ring4Sum(
            kit,
            sem + 8 * NP + 12 * p,
            lambda d, h, t, at, p=p: part[up(zh, d), core, p, h, at, :]
            + pair[up(zh, d), p, h, at, :],
            1,
            RP,
            16,
            (zcode.at[p, 0], zcode.at[p, 1]),
            (sides.at[p, 0, 0], sides.at[p, 0, 1], cols.at[0]),
            dev_zh(1),
            dev_zh(3),
        )
        for p in range(NP)
    ]
    def logits_begin(p):
        for h in (0, 1):
            pair_in(2, p, h)
            zr[p].send(h)

    forward(2, 0)
    forward(2, 1)
    logits_begin(0)
    forward(3, 1)
    pair_in(3, 0, 1)
    zr[0].send(2)
    forward(1, 0)
    pair_in(1, 0, 0)
    zr[0].send(3)
    forward(3, 0)
    forward(1, 1)
    pair_in(3, 0, 0)
    pair_in(1, 0, 1)
    zr[0].relay()
    logits_begin(1)
    pair_in(3, 1, 1)
    zr[1].send(2)
    pair_in(1, 1, 0)
    zr[1].send(3)
    forward(0, 0)
    forward(0, 1)
    pair_in(3, 1, 0)
    pair_in(1, 1, 1)
    sem2 = sem + 8 * NP + 12 * NP

    lanes = lax.broadcasted_iota(jnp.int32, (16, 128), 1)
    cols0 = lax.broadcasted_iota(jnp.int32, (16, HV), 1) + v * VL

    def peer_copy(p, r):
        return pltpu.make_async_remote_copy(
            src_ref=msg.at[p],
            dst_ref=peers.at[p, r - 1],
            send_sem=st_s.at[p, r - 1],
            recv_sem=st_r.at[p, r - 1],
            device_id=(c, (v + r) % NV),
            device_id_type=pl.DeviceIdType.MESH,
        )

    def softmax(p):
        for h in (0, 1):
            pair_in(0, p, h)
        zr[p].arrive()

        @pl.loop(0, RP // 16)
        def _(r):
            at = pl.ds(pl.multiple_of(r * 16, 16), 16)
            t = tcol[pl.ds(pl.multiple_of(p * RP + r * 16, 16), 16), :]
            l0 = zr[p].total(0, 0, at)
            l1 = zr[p].total(1, 0, at)
            top = jnp.maximum(
                jnp.max(l0, axis=1, keepdims=True), jnp.max(l1, axis=1, keepdims=True)
            )
            hit = jnp.sum(jnp.where(cols0 == t, l0, 0.0), axis=1, keepdims=True) + jnp.sum(
                jnp.where(cols0 + HV == t, l1, 0.0), axis=1, keepdims=True
            )
            e0 = jnp.exp(l0 - top)
            e1 = jnp.exp(l1 - top)
            total = jnp.sum(e0, axis=1, keepdims=True) + jnp.sum(e1, axis=1, keepdims=True)
            logit[p, 0, at, :] = e0
            logit[p, 1, at, :] = e1
            stat[at, :] = jnp.where(lanes == 0, top, jnp.where(lanes == 1, total, hit))

        msg[p] = jnp.transpose(stat[...])[:8]

        @pl.loop(1, NV)
        def _(r):
            peer_copy(p, r).start()

    def gradient(p):
        @pl.loop(1, NV)
        def _(r):
            peer_copy(p, r).wait_recv()

        top, total, hit = msg[p, 0:1, :], msg[p, 1:2, :], msg[p, 2:3, :]
        tops = peers[p, :, 0, :]
        best = jnp.maximum(top, jnp.max(tops, axis=0, keepdims=True))
        everyone = total * jnp.exp(top - best) + jnp.sum(
            peers[p, :, 1, :] * jnp.exp(tops - best), axis=0, keepdims=True
        )
        hits = hit + jnp.sum(peers[p, :, 2, :], axis=0, keepdims=True)
        loss = jnp.log(everyone) + best - hits
        scale = jnp.exp(top - best) / everyone
        odd = lax.broadcasted_iota(jnp.int32, (128, 128), 0) % 2 == 1
        lcol[...] = jnp.transpose(jnp.where(odd, loss, scale))
        spot = lax.broadcasted_iota(jnp.int32, (RP, ROWS // 2), 1) * 2
        line = lax.broadcasted_iota(jnp.int32, (RP, ROWS // 2), 0) + p * RP
        for d in (0, 1):
            found = jnp.sum(
                jnp.where(line == spot + d, lcol[:RP, 1:2], 0.0), axis=0, keepdims=True
            )
            loss_out[d : d + 1, :] = found if p == 0 else loss_out[d : d + 1, :] + found

        @pl.loop(0, RP // 16)
        def _(r):
            at = pl.ds(pl.multiple_of(r * 16, 16), 16)
            here = pl.ds(pl.multiple_of(p * RP + r * 16, 16), 16)
            t = tcol[here, :]
            w = wcol[here, :]
            s = lcol[at, 0:1]
            for h in (0, 1):
                one = (cols0 + h * HV == t).astype(F32)
                dl[zh, core, here, h * HV : (h + 1) * HV] = (
                    w * (logit[p, h, at, :] * s - one)
                ).astype(BF16)

    class Gather:
        def __init__(self, p):
            self.p, self.base = p, sem2 + 9 * p
            self.all = pl.ds(p * RP, RP)
            self.first = pl.ds(p * RP, RP // 2)
            self.last = pl.ds(p * RP + RP // 2, RP // 2)

        def go(self, d, k, rows, i, dev):
            slot = dl.at[up(zh, d), k, rows]
            start(slot, slot, self.base + i, dev)

        def come(self, d, k, rows, i):
            slot = dl.at[up(zh, d), k, rows]
            rdma(slot, slot, self.base + i, partner).wait_recv()

        def begin(self):
            self.go(0, core, self.all, 0, dev_zh(1))
            self.go(0, core, self.all, 1, dev_zh(3))
            self.go(0, core, self.all, 2, partner)

        def near(self):
            self.come(3, core, self.all, 0)
            self.go(3, core, self.first, 3, dev_zh(1))
            self.come(1, core, self.all, 1)
            self.go(1, core, self.last, 5, dev_zh(3))
            self.go(3, core, self.all, 4, partner)
            self.go(1, core, self.all, 6, partner)

        def far(self):
            self.come(2, core, self.first, 3)
            self.go(2, core, self.first, 7, partner)
            self.come(2, core, self.last, 5)
            self.go(2, core, self.last, 8, partner)

        def backward(self, *ds):
            other = 1 - core
            for d in ds:
                if d == 2:
                    self.come(2, other, self.first, 7)
                    self.come(2, other, self.last, 8)
                else:
                    self.come(d, other, self.all, {0: 2, 3: 4, 1: 6}[d])
            lhs = [dl[up(zh, d), k, self.all] for d in ds for k in (0, 1)]
            lhs = jnp.concatenate(lhs, axis=0)
            for j in range(4):
                res = lax.dot_general(
                    lhs,
                    head[j * WIDTH : (j + 1) * WIDTH, :],
                    (((1,), (1,)), ((), ())),
                    preferred_element_type=F32,
                )
                for i, d in enumerate(ds):
                    at = up(up(zh, d), zh)
                    for k in (0, 1):
                        lo = (2 * i + k) * RP
                        g[at, 2 * k + j // 2, j % 2, self.all] = res[lo : lo + RP]

    class Collect:
        def __init__(self, p):
            self.p = p
            base = sem2 + 9 * NP + 32 * p
            self.base = base

            def here(at, lo=0):
                return pl.ds(p * RP + lo + at.start, at.size)

            self.here = here

            def ring(i, k, value, tiles, rows, code, dev):
                return Ring4Sum(
                    kit,
                    base + 12 * i,
                    value,
                    tiles,
                    rows,
                    rows,
                    (code.at[p, k, 0], code.at[p, k, 1]),
                    (sides.at[p, 1 + i, 0], sides.at[p, 1 + i, 1], cols.at[1 + k]),
                    dev(1),
                    dev(3),
                )

            rows = pl.ds(p * RP, RP)
            if p in PLAIN:
                self.one = (
                    PlainSum(
                        kit,
                        base,
                        lambda d, h: g.at[pl.ds(up(2 * h, 2 * zh), 2), up(y, d), 0, rows],
                        land1.at[p, 0],
                        dev_y(1),
                        dev_y(3),
                    ),
                    PlainSum(
                        kit,
                        base + 12,
                        lambda d, h: g.at[up(x, d), pl.ds(2 * h, 2), 1, rows],
                        land1.at[p, 1],
                        dev_x(1),
                        dev_x(3),
                    ),
                )
                return
            self.one = (
                ring(0, 0, lambda d, h, t, at: g[up(2 * h + t, 2 * zh), up(y, d), 0, here(at), :], 2, RP, code1, dev_y),
                ring(1, 1, lambda d, h, t, at: g[up(x, d), 2 * h + t, 1, here(at), :], 2, RP, code1, dev_x),
            )

        def straight(self, k, d):
            rows = pl.ds(self.p * RP, RP)
            if k == 0:
                src, dev = g.at[up(x, d), y, 0, rows], dev_x(d)
            else:
                src, dev = g.at[x, up(y, d), 1, rows], dev_y(d)
            return src, land2.at[self.p, k, d - 1], self.base + 24 + 3 * k + d - 1, dev

        def begin_two(self):
            for d in (2, 1, 3):
                for k in (0, 1):
                    start(*self.straight(k, d))

        def begin(self, stage):
            for i in (0, 1, 2, 3):
                for s in stage:
                    s.send(i)

        def begin_early(self):
            for i in (0, 3):
                self.one[0].send(i)

        def begin_late(self):
            self.one[0].send(1)
            self.one[1].send(0)
            self.one[0].send(2)
            for i in (1, 2, 3):
                self.one[1].send(i)

        def relay(self, stage):
            for s in stage:
                s.relay()

        def end_one(self):
            for k, s in enumerate(self.one):
                s.arrive()

                at = pl.ds(0, RP)
                for h in (0, 1):
                    for t in (0, 1):
                        val = s.total(h, t, at)
                        if k == 0:
                            g[up(2 * h + t, 2 * zh), y, 0, self.here(at), :] = val
                        else:
                            g[x, 2 * h + t, 1, self.here(at), :] = val

        def end_two(self):
            for k in (0, 1):
                for d in (1, 2, 3):
                    rdma(*self.straight(k, d)).wait_recv()
            for k in (0, 1):
                rows = pl.ds(self.p * RP, RP)
                total = g[x, y, k, rows]
                for d in range(3):
                    total = total + land2[self.p, k, d]
                g[x, y, k, rows] = total

            rows = pl.ds(self.p * RP, RP)
            start(g.at[x, y, 1 - zl, rows], zbuf.at[self.p], self.base + 30, dev_zl)

        def out(self):
            rows = pl.ds(self.p * RP, RP)
            rdma(g.at[x, y, 1 - zl, rows], zbuf.at[self.p], self.base + 30, dev_zl).wait_recv()
            obuf[self.p] = (g[x, y, zl, rows] + zbuf[self.p]).astype(BF16)
            src, dst = obuf.at[self.p], grad_out.at[rows]

            @pl.when(is_self)
            def _():
                pltpu.make_async_copy(src, dst, lsem.at[2 + self.p]).start()

            @pl.when(jnp.logical_not(is_self))
            def _():
                rdma(src, dst, self.base + 31, owner).start()

        def done(self):
            rows = pl.ds(self.p * RP, RP)
            src, dst = obuf.at[self.p], grad_out.at[rows]

            @pl.when(is_self)
            def _():
                pltpu.make_async_copy(src, dst, lsem.at[2 + self.p]).wait()

            @pl.when(jnp.logical_not(is_self))
            def _():
                rdma(src, dst, self.base + 31, owner).wait()

    def peers_sent(p):
        @pl.loop(1, NV)
        def _(r):
            peer_copy(p, r).wait_send()

    ga, gb = Gather(0), Gather(1)
    ea, eb = Collect(0), Collect(1)
    softmax(0)
    zr[1].relay()
    gradient(0)
    ga.begin()
    softmax(1)
    ga.backward(0)
    ga.near()
    gradient(1)
    early = len(kit.pending)
    gb.begin()
    ga.backward(3, 1)
    ga.far()
    ga.backward(2)
    ea.begin(ea.one)
    gb.backward(0)
    ea.relay(ea.one)
    gb.near()
    for cp in kit.pending[:early]:
        cp.wait_send()
    del kit.pending[:early]
    peers_sent(0)
    ea.end_one()
    ea.begin_two()
    gb.backward(3, 1)
    gb.far()
    peers_sent(1)
    eb.begin_early()
    gb.backward(2)
    eb.begin_late()
    ea.end_two()
    eb.relay(eb.one)
    ea.out()
    eb.end_one()
    eb.begin_two()
    eb.end_two()
    eb.out()
    ea.done()
    eb.done()

    for cp in kit.pending:
        cp.wait_send()


NSEM = 34 + 8 * NP + 12 * NP + 9 * NP + 32 * NP


def body(hidden, head, targets, loss_weight):
    tile = (ROWS, WIDTH)
    vmem = pl.BlockSpec(memory_space=pltpu.VMEM)
    loss, grad = pl.pallas_call(
        kernel,
        out_shape=(
            jax.ShapeDtypeStruct((2, ROWS // 2), F32),
            jax.ShapeDtypeStruct(tile, BF16),
        ),
        in_specs=[vmem, pl.BlockSpec(memory_space=pl.ANY), vmem, vmem],
        out_specs=(vmem, pl.BlockSpec(memory_space=pl.ANY)),
        scratch_shapes=[
            pltpu.VMEM((RING, RING, 2, *tile), BF16),
            pltpu.VMEM((SLAB, VL), BF16),
            pltpu.VMEM((RING, 2, NP, 2, RP, HV), F32),
            pltpu.VMEM((RING, NP, 2, RP, HV), F32),
            pltpu.VMEM((NP, 2, 6, 1, RP, HV), I16),
            pltpu.VMEM((NP, 2, RP, HV), F32),
            pltpu.VMEM((ROWS, 128), F32),
            pltpu.VMEM((ROWS, 1), jnp.int32),
            pltpu.VMEM((ROWS, 1), F32),
            pltpu.VMEM((ROWS, 128), F32),
            pltpu.VMEM((NP, 8, ROWS), F32),
            pltpu.VMEM((NP, NV - 1, 8, ROWS), F32),
            pltpu.VMEM((RING, 2, ROWS, VL), BF16),
            pltpu.VMEM((RING, RING, 2, *tile), F32),
            pltpu.VMEM((NP, 2, 2, 6, 2, RP, WIDTH), I16),
            pltpu.VMEM((NP, 2, 6, 2, RP, WIDTH), F32),
            pltpu.VMEM((NP, 2, 3, RP, WIDTH), F32),
            pltpu.VMEM((NP, 3, 2, 6, 8, 128), F32),
            pltpu.VMEM((3, 6, 128, 128), F32),
            pltpu.VMEM((NP, RP, WIDTH), F32),
            pltpu.VMEM((NP, RP, WIDTH), BF16),
            pltpu.VMEM(tile, BF16),
            pltpu.SemaphoreType.DMA((NSEM,)),
            pltpu.SemaphoreType.DMA((NSEM,)),
            pltpu.SemaphoreType.DMA((NP, NV - 1)),
            pltpu.SemaphoreType.DMA((NP, NV - 1)),
            pltpu.SemaphoreType.DMA((2 + NP,)),
        ],
        compiler_params=pltpu.CompilerParams(
            collective_id=0, has_side_effects=True, vmem_limit_bytes=60 * 1024 * 1024
        ),
        name="mtp_loss",
    )(hidden, head, targets.T, loss_weight.T)
    rows, depths = targets.shape
    return loss.T, grad.reshape(rows, depths, WIDTH)


def solution(mesh):
    return jax.shard_map(
        body,
        mesh=mesh,
        in_specs=(P("ctx", None, "vocab"), P("ctx", "vocab"), P("ctx", None), P("ctx", None)),
        out_specs=(P("ctx", None), P("ctx", None, "vocab")),
        check_vma=False,
    )
```

```python
import jax
import jax.numpy as jnp
from jax import lax
from jax.experimental import pallas as pl
from jax.experimental.pallas import tpu as pltpu
from jax.sharding import PartitionSpec as P

F32 = jnp.float32
BF16 = jnp.bfloat16
RING = 4
NV = 32
ROWS = 128
WIDTH = 224
VL = 2048
HV = VL // 2
SLAB = 4 * WIDTH
NP = 2
PLAIN = (0,)
RP = ROWS // NP
I16 = jnp.int16
LEVELS = 32766.0
HOPS = ((2, 0, 0), (2, 1, 1), (3, 1, 0), (1, 0, 1), (3, 0, 0), (1, 1, 1))


class Ring4Sum:
    def __init__(self, k, base, value, tiles, rows, block, coded, sides, plus, minus):
        self.k, self.base, self.value = k, base, value
        self.tiles, self.rows, self.block = tiles, rows, block
        (self.out, self.land), (self.sout, self.sland, self.cols) = coded, sides
        self.plus, self.minus = plus, minus

    def copies(self, i):
        dev = self.plus if HOPS[i][2] else self.minus
        b = self.base + 2 * i
        return (
            self.k.rdma(self.out.at[i], self.land.at[i], b, dev),
            self.k.rdma(self.sout.at[i], self.sland.at[i], b + 1, dev),
        )

    def send(self, i, landed=()):
        d, h, _ = HOPS[i]
        stat = self.k.stat
        lanes = lax.broadcasted_iota(jnp.int32, (self.block, 128), 1)

        for r in range(self.rows // self.block):
            at = pl.ds(r * self.block, self.block)
            side = jnp.zeros((self.block, 128), F32)
            for t in range(self.tiles):
                val = self.value(d, h, t, at)
                for j in landed:
                    val = val + self.decoded(j, t, at)
                low = jnp.min(val, axis=1, keepdims=True)
                high = jnp.max(val, axis=1, keepdims=True)
                middle = 0.5 * low + 0.5 * high
                span = jnp.maximum(0.5 * high - 0.5 * low, 1e-30)
                steps = jnp.clip(jnp.round((val - middle) * (LEVELS / span)), -LEVELS, LEVELS)
                self.out[i, t, at, :] = steps.astype(jnp.int32).astype(I16)
                side = jnp.where(lanes == 2 * t, middle, side)
                side = jnp.where(lanes == 2 * t + 1, span * (1.0 / LEVELS), side)
            stat[at, :] = side

        self.sout[i] = jnp.transpose(stat[...])[:8]
        for cp in self.copies(i):
            cp.start()
            self.k.pending.append(cp)

    def receive(self, i):
        for cp in self.copies(i):
            cp.wait_recv()
        rows = jnp.concatenate([self.sland[i]] * 16, axis=0)
        self.cols[i] = jnp.transpose(rows)

    def decoded(self, i, t, at):
        steps = self.land[i, t, at, :].astype(jnp.int32).astype(F32)
        return steps * self.cols[i, at, 2 * t + 1 : 2 * t + 2] + self.cols[i, at, 2 * t : 2 * t + 1]

    def relay(self):
        self.receive(0)
        self.send(4, (0,))
        self.receive(1)
        self.send(5, (1,))

    def arrive(self):
        for i in (2, 3, 4, 5):
            self.receive(i)

    def total(self, h, t, at):
        i, j = ((3, 4), (2, 5))[h]
        return self.value(0, h, t, at) + self.decoded(i, t, at) + self.decoded(j, t, at)


class PlainSum(Ring4Sum):
    def __init__(self, k, base, part, land, plus, minus):
        self.k, self.base, self.part, self.land = k, base, part, land
        self.plus, self.minus = plus, minus

    def copies(self, i):
        d, h, to_plus = HOPS[i]
        dev = self.plus if to_plus else self.minus
        return (self.k.rdma(self.part(d, h), self.land.at[i], self.base + 2 * i, dev),)

    def send(self, i, landed=()):
        part = self.part(*HOPS[i][:2])
        for j in landed:
            part[...] = part[...] + self.land[j]
        for cp in self.copies(i):
            cp.start()
            self.k.pending.append(cp)

    def receive(self, i):
        for cp in self.copies(i):
            cp.wait_recv()

    def total(self, h, t, at):
        i, j = ((3, 4), (2, 5))[h]
        return self.part(0, h)[t, at, :] + self.land[i, t, at, :] + self.land[j, t, at, :]


class Tools:
    def __init__(self, ssem, rsem, stat):
        self.ssem, self.rsem, self.stat, self.pending = ssem, rsem, stat, []

    def rdma(self, src, dst, i, dev):
        return pltpu.make_async_remote_copy(
            src_ref=src,
            dst_ref=dst,
            send_sem=self.ssem.at[i],
            recv_sem=self.rsem.at[i],
            device_id=dev,
            device_id_type=pl.DeviceIdType.MESH,
        )

    def start(self, src, dst, i, dev):
        cp = self.rdma(src, dst, i, dev)
        cp.start()
        self.pending.append(cp)


def kernel(
    hid,
    head_hbm,
    tgt,
    wgt,
    loss_out,
    grad_out,
    buf,
    head,
    part,
    pair,
    zcode,
    logit,
    stat,
    tcol,
    wcol,
    lcol,
    msg,
    peers,
    dl,
    g,
    code1,
    land1,
    land2,
    sides,
    cols,
    zbuf,
    obuf,
    flat,
    ssem,
    rsem,
    st_s,
    st_r,
    lsem,
):
    c = lax.axis_index("ctx")
    v = lax.axis_index("vocab")
    zh, core = c // 2, c % 2
    x, y, zl = v // 8, (v // 2) % 4, v % 2
    kit = Tools(ssem, rsem, stat)
    rdma, start = kit.rdma, kit.start

    def up(i, d):
        return (i + d) % RING

    def dev_zh(d):
        return (up(zh, d) * 2 + core, v)

    def dev_x(d):
        return (c, up(x, d) * 8 + y * 2 + zl)

    def dev_y(d):
        return (c, x * 8 + up(y, d) * 2 + zl)

    partner = (zh * 2 + 1 - core, v)
    dev_zl = (c, x * 8 + y * 2 + 1 - zl)
    hx, hy = up(x, zh), core * 2 + y % 2
    holder = (v // 4, hx * 8 + hy * 2 + zl)
    owner = (up(x, 4 - zh) * 2 + y // 2, 4 * c + v % 4)
    is_self = jnp.logical_and(holder[0] == c, holder[1] == v)

    head_copy = pltpu.make_async_copy(head_hbm, head, lsem.at[0])
    head_copy.start()

    barrier = pltpu.get_barrier_semaphore()

    def greet(dev):
        pl.semaphore_signal(barrier, inc=1, device_id=dev, device_id_type=pl.DeviceIdType.MESH)

    @pl.when(jnp.logical_not(is_self))
    def _():
        greet(holder)
        greet(owner)

    for dev in (
        partner,
        dev_zh(1),
        dev_zh(3),
        dev_x(1),
        dev_x(3),
        dev_y(1),
        dev_y(3),
        dev_zl,
    ):
        greet(dev)

    flat[...] = hid[...].reshape(ROWS, WIDTH)

    @pl.when(jnp.logical_not(is_self))
    def _():
        pl.semaphore_wait(barrier, 10)

    @pl.when(is_self)
    def _():
        pl.semaphore_wait(barrier, 8)

    @pl.when(is_self)
    def _():
        cp = pltpu.make_async_copy(flat, buf.at[x, y, zl], lsem.at[1])
        cp.start()
        cp.wait()

    @pl.when(jnp.logical_not(is_self))
    def _():
        cp = rdma(flat, buf.at[hx, hy, zl], 0, holder)
        cp.start()
        cp.wait_send()
        rdma(flat, buf.at[x, y, zl], 0, holder).wait_recv()

    start(buf.at[x, y, zl], buf.at[x, y, zl], 1, dev_zl)

    row = lax.broadcasted_iota(jnp.int32, (ROWS, ROWS // 2), 0)
    tok = lax.broadcasted_iota(jnp.int32, (ROWS, ROWS // 2), 1)

    def as_column(pairs):
        both = jnp.where(row % 2 == 1, pairs[1:2, :], pairs[0:1, :])
        return jnp.sum(jnp.where(row // 2 == tok, both, 0.0), axis=1, keepdims=True)

    tcol[...] = as_column(tgt[...].astype(F32)).astype(jnp.int32)
    wcol[...] = as_column(wgt[...])

    lines = (
        (lambda a, b: buf.at[a, b, 0], x, y, dev_x, dev_y),
        (lambda a, b: buf.at[b, a, 1], y, x, dev_y, dev_x),
    )
    steps = (0, 3, 1, 2)

    def second(k, n):
        at, a, b, dev_a, dev_b = lines[k]
        base = 2 + 16 * k
        for d, o in ((1, 4), (3, 8)):
            tile = at(up(a, steps[n]), b)
            start(tile, tile, base + o + n, dev_b(d))

    def second_in(k, n, d):
        at, a, b, dev_a, dev_b = lines[k]
        base = 2 + 16 * k
        tile = at(up(a, steps[n]), up(b, 4 - d))
        rdma(tile, tile, base + (4 if d == 1 else 8) + n, dev_b(d)).wait_recv()
        return tile

    def first(k):
        at, a, b, dev_a, dev_b = lines[k]
        base = 2 + 16 * k
        tile = at(a, b)
        return [
            rdma(tile, tile, base + i, dev)
            for i, dev in ((0, dev_a(1)), (1, dev_a(3)), (4, dev_b(1)), (8, dev_b(3)))
        ]

    def start_first(k):
        for cp in first(k):
            cp.start()

    for k in (0, 1):
        kit.pending.extend(first(k))
        pl.when(zl == k)(lambda: start_first(k))
    rdma(buf.at[x, y, zl], buf.at[x, y, 1 - zl], 1, dev_zl).wait_recv()
    for k in (1, 0):
        pl.when(zl != k)(lambda: start_first(k))
    for k, (at, a, b, dev_a, dev_b) in enumerate(lines):
        base = 2 + 16 * k
        for d, i, rows in ((1, 0, pl.ds(0, 64)), (3, 1, pl.ds(64, 64))):
            tile = at(up(a, 4 - d), b)
            rdma(tile, tile, base + i, dev_a(d)).wait_recv()
            half = tile.at[rows]
            start(half, half, base + 2 + i, dev_a(d))
            second(k, 1 + i)
    for k, (at, a, b, dev_a, dev_b) in enumerate(lines):
        base = 2 + 16 * k
        for d, i, rows in ((1, 0, pl.ds(0, 64)), (3, 1, pl.ds(64, 64))):
            half = at(up(a, 2), b).at[rows]
            rdma(half, half, base + 2 + i, dev_a(d)).wait_recv()
        second(k, 3)
    for n, d in ((0, 1), (1, 1), (2, 3), (3, 3)):
        for k, (at, a, b, dev_a, dev_b) in enumerate(lines):
            tile = second_in(k, n, d)
            start(tile, tile, 2 + 16 * k + 12 + n, dev_b(d))
    for k, (at, a, b, dev_a, dev_b) in enumerate(lines):
        for n, d in ((2, 1), (3, 1), (0, 3), (1, 3)):
            second_in(k, n, d)
        for n in range(4):
            tile = at(up(a, steps[n]), up(b, 2))
            rdma(tile, tile, 2 + 16 * k + 12 + n, dev_b(1)).wait_recv()
    sem = 34

    head_copy.wait()

    def forward(d, h):
        q = up(zh, d)
        at = up(q, zh)

        @pl.loop(0, HV // 256)
        def _(n):
            cs = pl.ds(pl.multiple_of(h * HV + n * 256, 256), 256)
            out_cs = pl.ds(pl.multiple_of(n * 256, 256), 256)
            acc = None
            for j in range(4):
                lhs = jnp.concatenate([buf[at, j // 2, j % 2], buf[at, 2 + j // 2, j % 2]], axis=0)
                term = jnp.dot(
                    lhs, head[j * WIDTH : (j + 1) * WIDTH, cs], preferred_element_type=F32
                )
                acc = term if acc is None else acc + term
            for k in range(2):
                for p in range(NP):
                    lo = k * ROWS + p * RP
                    part[q, k, p, h, :, out_cs] = acc[lo : lo + RP]

        for p in range(NP):
            start(part.at[q, 1 - core, p, h], pair.at[q, p, h], pair_sem(d, p, h), partner)

    def pair_sem(d, p, h):
        return sem + (d * NP + p) * 2 + h

    def pair_in(d, p, h):
        q = up(zh, d)
        rdma(part.at[q, 1 - core, p, h], pair.at[q, p, h], pair_sem(d, p, h), partner).wait_recv()

    zr = [
        Ring4Sum(
            kit,
            sem + 8 * NP + 12 * p,
            lambda d, h, t, at, p=p: part[up(zh, d), core, p, h, at, :]
            + pair[up(zh, d), p, h, at, :],
            1,
            RP,
            16,
            (zcode.at[p, 0], zcode.at[p, 1]),
            (sides.at[p, 0, 0], sides.at[p, 0, 1], cols.at[0]),
            dev_zh(1),
            dev_zh(3),
        )
        for p in range(NP)
    ]
    def logits_begin(p):
        for h in (0, 1):
            pair_in(2, p, h)
            zr[p].send(h)

    forward(2, 0)
    forward(2, 1)
    logits_begin(0)
    forward(3, 1)
    pair_in(3, 0, 1)
    zr[0].send(2)
    forward(1, 0)
    pair_in(1, 0, 0)
    zr[0].send(3)
    forward(3, 0)
    forward(1, 1)
    pair_in(3, 0, 0)
    pair_in(1, 0, 1)
    zr[0].relay()
    logits_begin(1)
    pair_in(3, 1, 1)
    zr[1].send(2)
    pair_in(1, 1, 0)
    zr[1].send(3)
    forward(0, 0)
    forward(0, 1)
    pair_in(3, 1, 0)
    pair_in(1, 1, 1)
    sem2 = sem + 8 * NP + 12 * NP

    lanes = lax.broadcasted_iota(jnp.int32, (16, 128), 1)
    cols0 = lax.broadcasted_iota(jnp.int32, (16, HV), 1) + v * VL

    def peer_copy(p, r):
        return pltpu.make_async_remote_copy(
            src_ref=msg.at[p],
            dst_ref=peers.at[p, r - 1],
            send_sem=st_s.at[p, r - 1],
            recv_sem=st_r.at[p, r - 1],
            device_id=(c, (v + r) % NV),
            device_id_type=pl.DeviceIdType.MESH,
        )

    def softmax(p):
        for h in (0, 1):
            pair_in(0, p, h)
        zr[p].arrive()

        @pl.loop(0, RP // 16)
        def _(r):
            at = pl.ds(pl.multiple_of(r * 16, 16), 16)
            t = tcol[pl.ds(pl.multiple_of(p * RP + r * 16, 16), 16), :]
            l0 = zr[p].total(0, 0, at)
            l1 = zr[p].total(1, 0, at)
            top = jnp.maximum(
                jnp.max(l0, axis=1, keepdims=True), jnp.max(l1, axis=1, keepdims=True)
            )
            hit = jnp.sum(jnp.where(cols0 == t, l0, 0.0), axis=1, keepdims=True) + jnp.sum(
                jnp.where(cols0 + HV == t, l1, 0.0), axis=1, keepdims=True
            )
            e0 = jnp.exp(l0 - top)
            e1 = jnp.exp(l1 - top)
            total = jnp.sum(e0, axis=1, keepdims=True) + jnp.sum(e1, axis=1, keepdims=True)
            logit[p, 0, at, :] = e0
            logit[p, 1, at, :] = e1
            stat[at, :] = jnp.where(lanes == 0, top, jnp.where(lanes == 1, total, hit))

        msg[p] = jnp.transpose(stat[...])[:8]

        @pl.loop(1, NV)
        def _(r):
            peer_copy(p, r).start()

    def gradient(p):
        @pl.loop(1, NV)
        def _(r):
            peer_copy(p, r).wait_recv()

        top, total, hit = msg[p, 0:1, :], msg[p, 1:2, :], msg[p, 2:3, :]
        tops = peers[p, :, 0, :]
        best = jnp.maximum(top, jnp.max(tops, axis=0, keepdims=True))
        everyone = total * jnp.exp(top - best) + jnp.sum(
            peers[p, :, 1, :] * jnp.exp(tops - best), axis=0, keepdims=True
        )
        hits = hit + jnp.sum(peers[p, :, 2, :], axis=0, keepdims=True)
        loss = jnp.log(everyone) + best - hits
        scale = jnp.exp(top - best) / everyone
        odd = lax.broadcasted_iota(jnp.int32, (128, 128), 0) % 2 == 1
        lcol[...] = jnp.transpose(jnp.where(odd, loss, scale))
        spot = lax.broadcasted_iota(jnp.int32, (RP, ROWS // 2), 1) * 2
        line = lax.broadcasted_iota(jnp.int32, (RP, ROWS // 2), 0) + p * RP
        for d in (0, 1):
            found = jnp.sum(
                jnp.where(line == spot + d, lcol[:RP, 1:2], 0.0), axis=0, keepdims=True
            )
            loss_out[d : d + 1, :] = found if p == 0 else loss_out[d : d + 1, :] + found

        @pl.loop(0, RP // 16)
        def _(r):
            at = pl.ds(pl.multiple_of(r * 16, 16), 16)
            here = pl.ds(pl.multiple_of(p * RP + r * 16, 16), 16)
            t = tcol[here, :]
            w = wcol[here, :]
            s = lcol[at, 0:1]
            for h in (0, 1):
                one = (cols0 + h * HV == t).astype(F32)
                dl[zh, core, here, h * HV : (h + 1) * HV] = (
                    w * (logit[p, h, at, :] * s - one)
                ).astype(BF16)

    class Gather:
        def __init__(self, p):
            self.p, self.base = p, sem2 + 9 * p
            self.all = pl.ds(p * RP, RP)
            self.first = pl.ds(p * RP, RP // 2)
            self.last = pl.ds(p * RP + RP // 2, RP // 2)

        def go(self, d, k, rows, i, dev):
            slot = dl.at[up(zh, d), k, rows]
            start(slot, slot, self.base + i, dev)

        def come(self, d, k, rows, i):
            slot = dl.at[up(zh, d), k, rows]
            rdma(slot, slot, self.base + i, partner).wait_recv()

        def begin(self):
            self.go(0, core, self.all, 0, dev_zh(1))
            self.go(0, core, self.all, 1, dev_zh(3))
            self.go(0, core, self.all, 2, partner)

        def near(self):
            self.come(3, core, self.all, 0)
            self.go(3, core, self.first, 3, dev_zh(1))
            self.come(1, core, self.all, 1)
            self.go(1, core, self.last, 5, dev_zh(3))
            self.go(3, core, self.all, 4, partner)
            self.go(1, core, self.all, 6, partner)

        def far(self):
            self.come(2, core, self.first, 3)
            self.go(2, core, self.first, 7, partner)
            self.come(2, core, self.last, 5)
            self.go(2, core, self.last, 8, partner)

        def backward(self, *ds):
            other = 1 - core
            for d in ds:
                if d == 2:
                    self.come(2, other, self.first, 7)
                    self.come(2, other, self.last, 8)
                else:
                    self.come(d, other, self.all, {0: 2, 3: 4, 1: 6}[d])
            lhs = [dl[up(zh, d), k, self.all] for d in ds for k in (0, 1)]
            lhs = jnp.concatenate(lhs, axis=0)
            for j in range(4):
                res = lax.dot_general(
                    lhs,
                    head[j * WIDTH : (j + 1) * WIDTH, :],
                    (((1,), (1,)), ((), ())),
                    preferred_element_type=F32,
                )
                for i, d in enumerate(ds):
                    at = up(up(zh, d), zh)
                    for k in (0, 1):
                        lo = (2 * i + k) * RP
                        g[at, 2 * k + j // 2, j % 2, self.all] = res[lo : lo + RP]

    class Collect:
        def __init__(self, p):
            self.p = p
            base = sem2 + 9 * NP + 32 * p
            self.base = base

            def here(at, lo=0):
                return pl.ds(p * RP + lo + at.start, at.size)

            self.here = here

            def ring(i, k, value, tiles, rows, code, dev):
                return Ring4Sum(
                    kit,
                    base + 12 * i,
                    value,
                    tiles,
                    rows,
                    rows,
                    (code.at[p, k, 0], code.at[p, k, 1]),
                    (sides.at[p, 1 + i, 0], sides.at[p, 1 + i, 1], cols.at[1 + k]),
                    dev(1),
                    dev(3),
                )

            rows = pl.ds(p * RP, RP)
            if p in PLAIN:
                self.one = (
                    PlainSum(
                        kit,
                        base,
                        lambda d, h: g.at[pl.ds(up(2 * h, 2 * zh), 2), up(y, d), 0, rows],
                        land1.at[p, 0],
                        dev_y(1),
                        dev_y(3),
                    ),
                    PlainSum(
                        kit,
                        base + 12,
                        lambda d, h: g.at[up(x, d), pl.ds(2 * h, 2), 1, rows],
                        land1.at[p, 1],
                        dev_x(1),
                        dev_x(3),
                    ),
                )
                return
            self.one = (
                ring(0, 0, lambda d, h, t, at: g[up(2 * h + t, 2 * zh), up(y, d), 0, here(at), :], 2, RP, code1, dev_y),
                ring(1, 1, lambda d, h, t, at: g[up(x, d), 2 * h + t, 1, here(at), :], 2, RP, code1, dev_x),
            )

        def straight(self, k, d):
            rows = pl.ds(self.p * RP, RP)
            if k == 0:
                src, dev = g.at[up(x, d), y, 0, rows], dev_x(d)
            else:
                src, dev = g.at[x, up(y, d), 1, rows], dev_y(d)
            return src, land2.at[self.p, k, d - 1], self.base + 24 + 3 * k + d - 1, dev

        def begin_two(self):
            for d in (2, 1, 3):
                for k in (0, 1):
                    start(*self.straight(k, d))

        def begin(self, stage):
            for i in (0, 1, 2, 3):
                for s in stage:
                    s.send(i)

        def begin_early(self):
            for i in (0, 3):
                self.one[0].send(i)

        def begin_late(self):
            self.one[0].send(1)
            self.one[1].send(0)
            self.one[0].send(2)
            for i in (1, 2, 3):
                self.one[1].send(i)

        def relay(self, stage):
            for s in stage:
                s.relay()

        def end_one(self):
            for k, s in enumerate(self.one):
                s.arrive()

                at = pl.ds(0, RP)
                for h in (0, 1):
                    for t in (0, 1):
                        val = s.total(h, t, at)
                        if k == 0:
                            g[up(2 * h + t, 2 * zh), y, 0, self.here(at), :] = val
                        else:
                            g[x, 2 * h + t, 1, self.here(at), :] = val

        def end_two(self):
            for k in (0, 1):
                for d in (1, 2, 3):
                    rdma(*self.straight(k, d)).wait_recv()
            for k in (0, 1):
                rows = pl.ds(self.p * RP, RP)
                total = g[x, y, k, rows]
                for d in range(3):
                    total = total + land2[self.p, k, d]
                g[x, y, k, rows] = total

            rows = pl.ds(self.p * RP, RP)
            start(g.at[x, y, 1 - zl, rows], zbuf.at[self.p], self.base + 30, dev_zl)

        def out(self):
            rows = pl.ds(self.p * RP, RP)
            rdma(g.at[x, y, 1 - zl, rows], zbuf.at[self.p], self.base + 30, dev_zl).wait_recv()
            obuf[self.p] = (g[x, y, zl, rows] + zbuf[self.p]).astype(BF16)
            src, dst = obuf.at[self.p], grad_out.at[rows]

            @pl.when(is_self)
            def _():
                pltpu.make_async_copy(src, dst, lsem.at[2 + self.p]).start()

            @pl.when(jnp.logical_not(is_self))
            def _():
                rdma(src, dst, self.base + 31, owner).start()

        def done(self):
            rows = pl.ds(self.p * RP, RP)
            src, dst = obuf.at[self.p], grad_out.at[rows]

            @pl.when(is_self)
            def _():
                pltpu.make_async_copy(src, dst, lsem.at[2 + self.p]).wait()

            @pl.when(jnp.logical_not(is_self))
            def _():
                rdma(src, dst, self.base + 31, owner).wait()

    def peers_sent(p):
        @pl.loop(1, NV)
        def _(r):
            peer_copy(p, r).wait_send()

    ga, gb = Gather(0), Gather(1)
    ea, eb = Collect(0), Collect(1)
    softmax(0)
    zr[1].relay()
    gradient(0)
    ga.begin()
    softmax(1)
    ga.backward(0)
    ga.near()
    gradient(1)
    early = len(kit.pending)
    gb.begin()
    ga.backward(3, 1)
    ga.far()
    ga.backward(2)
    ea.begin(ea.one)
    gb.backward(0)
    ea.relay(ea.one)
    later = len(kit.pending) - early
    gb.near()
    for cp in kit.pending[:early]:
        cp.wait_send()
    del kit.pending[:early]
    peers_sent(0)
    ea.end_one()
    ea.begin_two()
    gb.backward(3, 1)
    gb.far()
    for cp in kit.pending[:later]:
        cp.wait_send()
    del kit.pending[:later]
    peers_sent(1)
    eb.begin_early()
    gb.backward(2)
    eb.begin_late()
    ea.end_two()
    eb.relay(eb.one)
    ea.out()
    eb.end_one()
    eb.begin_two()
    eb.end_two()
    eb.out()
    ea.done()
    eb.done()

    for cp in kit.pending:
        cp.wait_send()


NSEM = 34 + 8 * NP + 12 * NP + 9 * NP + 32 * NP


def body(hidden, head, targets, loss_weight):
    tile = (ROWS, WIDTH)
    vmem = pl.BlockSpec(memory_space=pltpu.VMEM)
    loss, grad = pl.pallas_call(
        kernel,
        out_shape=(
            jax.ShapeDtypeStruct((2, ROWS // 2), F32),
            jax.ShapeDtypeStruct(tile, BF16),
        ),
        in_specs=[vmem, pl.BlockSpec(memory_space=pl.ANY), vmem, vmem],
        out_specs=(vmem, pl.BlockSpec(memory_space=pl.ANY)),
        scratch_shapes=[
            pltpu.VMEM((RING, RING, 2, *tile), BF16),
            pltpu.VMEM((SLAB, VL), BF16),
            pltpu.VMEM((RING, 2, NP, 2, RP, HV), F32),
            pltpu.VMEM((RING, NP, 2, RP, HV), F32),
            pltpu.VMEM((NP, 2, 6, 1, RP, HV), I16),
            pltpu.VMEM((NP, 2, RP, HV), F32),
            pltpu.VMEM((ROWS, 128), F32),
            pltpu.VMEM((ROWS, 1), jnp.int32),
            pltpu.VMEM((ROWS, 1), F32),
            pltpu.VMEM((ROWS, 128), F32),
            pltpu.VMEM((NP, 8, ROWS), F32),
            pltpu.VMEM((NP, NV - 1, 8, ROWS), F32),
            pltpu.VMEM((RING, 2, ROWS, VL), BF16),
            pltpu.VMEM((RING, RING, 2, *tile), F32),
            pltpu.VMEM((NP, 2, 2, 6, 2, RP, WIDTH), I16),
            pltpu.VMEM((NP, 2, 6, 2, RP, WIDTH), F32),
            pltpu.VMEM((NP, 2, 3, RP, WIDTH), F32),
            pltpu.VMEM((NP, 3, 2, 6, 8, 128), F32),
            pltpu.VMEM((3, 6, 128, 128), F32),
            pltpu.VMEM((NP, RP, WIDTH), F32),
            pltpu.VMEM((NP, RP, WIDTH), BF16),
            pltpu.VMEM(tile, BF16),
            pltpu.SemaphoreType.DMA((NSEM,)),
            pltpu.SemaphoreType.DMA((NSEM,)),
            pltpu.SemaphoreType.DMA((NP, NV - 1)),
            pltpu.SemaphoreType.DMA((NP, NV - 1)),
            pltpu.SemaphoreType.DMA((2 + NP,)),
        ],
        compiler_params=pltpu.CompilerParams(
            collective_id=0, has_side_effects=True, vmem_limit_bytes=60 * 1024 * 1024
        ),
        name="mtp_loss",
    )(hidden, head, targets.T, loss_weight.T)
    rows, depths = targets.shape
    return loss.T, grad.reshape(rows, depths, WIDTH)


def solution(mesh):
    return jax.shard_map(
        body,
        mesh=mesh,
        in_specs=(P("ctx", None, "vocab"), P("ctx", "vocab"), P("ctx", None), P("ctx", None)),
        out_specs=(P("ctx", None), P("ctx", None, "vocab")),
        check_vma=False,
    )
```
